256 devices in a mesh: row: 16 (over y_hi, x, core), col: 16 (over z, y_lo).
Axes of the slice: x: 4, y: 4 (y_hi: 2, y_lo: 2; y = y_hi * 2 + y_lo), z: 8, core: 2. Of those that a mesh axis runs over, the one named last changes fastest.
Arguments:
- factor_a: bfloat16 [128, 32768], P('row', 'col'), may hold values from -12 to 12
- factor_b: bfloat16 [128, 32768], P('row', 'col'), may hold values from -12 to 12
- pair: bfloat16 [1024, 1024, 128], P('row', 'col'), may hold values from -6 to 6
- proj_weight: bfloat16 [1024, 128], replicated, may hold values from -0.1875 to 0.1875
- proj_bias: float32 [128], replicated, may hold values from -3 to 3
- norm_gain: float32 [128], replicated, may hold values from 0.25 to 1.75
- norm_bias: float32 [128], replicated, may hold values from -3 to 3
- trans_in: bfloat16 [128, 1024], replicated, may hold values from -0.5 to 0.5
- trans_out: bfloat16 [512, 128], replicated, may hold values from -0.25 to 0.25
- cotangent: bfloat16 [1024, 1024, 128], P('row', 'col'), may hold values from -6 to 6
Outputs:
- new_pair: bfloat16 [1024, 1024, 128], P('row', 'col')
- pair_grad: bfloat16 [1024, 1024, 128], P('row', 'col')
- grad_a: float32 [128, 32768], P('row', 'col')
- grad_b: float32 [128, 32768], P('row', 'col')
The draws below stay inside these ranges and needn't reach their ends.
All inputs are finite; a program needn't handle non-finite values.
Results may differ from the reference program's by a relative error of at most 0.006.
Values may be sent and summed in bfloat16 or wider, within the bound.
A program may use at most 64 MiB of HBM per device.

```python
import jax
import jax.numpy as jnp
from jax import lax

H = 32
C = 128
F = 512
S = 128
R = 1024


def block_scale(own_key, dims, cuts, smallest, high):
    def one(position, shards_of):
        heights = jax.random.uniform(jax.random.fold_in(jax.random.fold_in(own_key, 6), position), (shards_of,), jnp.float32, smallest / len(cuts), high / len(cuts))
        return jnp.repeat(jnp.exp(heights), dims[position] // shards_of).reshape((-1,) + (1,) * (len(dims) - position - 1))

    level = one(*cuts[0])
    for cut in cuts[1:]:
        level = level * one(*cut)
    return level


def bell_draw(rng, dims, scale, bound, pieces=(), held_as=jnp.bfloat16):
    factor_of = block_scale(rng, dims, pieces, -0.22, 0.18) if pieces else 1.0
    drawn = jax.random.normal(rng, dims, jnp.float32) * scale * factor_of
    return jnp.minimum(jnp.maximum(drawn, -bound), bound).astype(held_as)


def setup_inputs(seed: int = 0) -> dict:
    streams_of = jax.random.split(jax.random.key(seed), 11)
    factor_a = bell_draw(streams_of[0], (S, R * H), 2.0, 12.0, ((0, 16), (1, 16)))
    factor_b = bell_draw(streams_of[1], (S, R * H), 2.0, 12.0, ((0, 16), (1, 16)))
    pair = bell_draw(streams_of[2], (R, R, C), 1.0, 6.0, ((0, 16), (1, 16)))
    proj_weight = bell_draw(streams_of[3], (H * H, C), (H * H) ** -0.5, 0.1875)
    proj_bias = bell_draw(streams_of[4], (C,), 0.5, 3.0, (), jnp.float32)
    norm_gain = jnp.clip(1.0 + 0.15 * jax.random.normal(streams_of[5], (C,), jnp.float32), 0.25, 1.75)
    norm_bias = bell_draw(streams_of[6], (C,), 0.5, 3.0, (), jnp.float32)
    trans_in = bell_draw(streams_of[7], (C, 2 * F), C ** -0.5, 0.5)
    trans_out = bell_draw(streams_of[8], (F, C), F ** -0.5, 0.25)
    cotangent = bell_draw(streams_of[9], (R, R, C), 1.0, 6.0, ((0, 16), (1, 16)))
    return dict(factor_a=factor_a, factor_b=factor_b, pair=pair, proj_weight=proj_weight, proj_bias=proj_bias, norm_gain=norm_gain, norm_bias=norm_bias, trans_in=trans_in, trans_out=trans_out, cotangent=cotangent)


def dot_last(left, right):
    return lax.dot_general(left, right, (((1,), (1,)), ((), ())), preferred_element_type=jnp.float32)

def dot_first(left, right):
    return lax.dot_general(left, right, (((0,), (0,)), ((), ())), preferred_element_type=jnp.float32)

def factor_pull(grad_rows, proj_weight, seq_count, hidden_dim):
    rows_i, cols_j, width = grad_rows.shape
    weight_cube = proj_weight.reshape(hidden_dim, hidden_dim, width).astype(jnp.float32)
    pulled = jnp.einsum('abc,hkc->ahbk', grad_rows.astype(jnp.float32), weight_cube) / seq_count
    pulled = pulled.astype(jnp.bfloat16)
    return pulled.reshape(rows_i * hidden_dim, cols_j * hidden_dim)

def pair_update(a_block, b_cols, pair_rows, cot_rows, proj_weight, proj_bias, norm_gain, norm_bias, trans_in, trans_out, seq_count, hidden_dim):
    rows_i, cols_j, width = pair_rows.shape
    units = trans_out.shape[0]
    outer = (dot_first(a_block, b_cols) / seq_count).astype(jnp.bfloat16)
    outer = outer.reshape(rows_i, hidden_dim, cols_j, hidden_dim).astype(jnp.float32)
    weight_cube = proj_weight.reshape(hidden_dim, hidden_dim, width).astype(jnp.float32)
    projected = jnp.einsum('ahbk,hkc->abc', outer, weight_cube).reshape(rows_i * cols_j, width)
    updated = pair_rows.reshape(rows_i * cols_j, width).astype(jnp.float32)
    updated = updated + projected + proj_bias
    row_mean = lax.optimization_barrier(jnp.mean(updated, axis=-1, keepdims=True))
    centered = updated - row_mean
    row_var = lax.optimization_barrier(jnp.mean(centered * centered, axis=-1, keepdims=True))
    inv_std = lax.rsqrt(row_var + 1e-05)
    normed = centered * inv_std
    lnorm = (normed * norm_gain + norm_bias).astype(jnp.bfloat16)
    both_pre = jnp.dot(lnorm, trans_in, preferred_element_type=jnp.float32)
    gate_pre = both_pre[:, :units]
    up_pre = both_pre[:, units:]
    sig_gate = jax.nn.sigmoid(gate_pre)
    activated = gate_pre * sig_gate
    hidden = (activated * up_pre).astype(jnp.bfloat16)
    new_rows = (updated + jnp.dot(hidden, trans_out, preferred_element_type=jnp.float32)).astype(jnp.bfloat16)
    cot_flat = cot_rows.reshape(rows_i * cols_j, width)
    d_hidden = dot_last(cot_flat, trans_out)
    d_gate = d_hidden * up_pre * sig_gate * (1.0 + gate_pre * (1.0 - sig_gate))
    d_up = d_hidden * activated
    d_both = jnp.concatenate([d_gate, d_up], axis=-1).astype(jnp.bfloat16)
    d_norm = dot_last(d_both, trans_in) * norm_gain
    d_mean = lax.optimization_barrier(jnp.mean(d_norm, axis=-1, keepdims=True))
    d_proj = lax.optimization_barrier(jnp.mean(d_norm * normed, axis=-1, keepdims=True))
    grad_flat = cot_flat.astype(jnp.float32) + inv_std * (d_norm - d_mean - normed * d_proj)
    grad_rows = grad_flat.astype(jnp.bfloat16).reshape(rows_i, cols_j, width)
    pulled = factor_pull(grad_rows, proj_weight, seq_count, hidden_dim)
    return (new_rows.reshape(rows_i, cols_j, width), grad_rows, pulled)

def reference(factor_a, factor_b, pair, proj_weight, proj_bias, norm_gain, norm_bias, trans_in, trans_out, cotangent):
    blocks = 32
    rows_block = R // blocks
    a_blocks = factor_a.reshape(S, blocks, rows_block * H).transpose(1, 0, 2)
    pair_blocks = pair.reshape(blocks, rows_block, R, C)
    cot_blocks = cotangent.reshape(blocks, rows_block, R, C)

    def advance(running, inputs_now):
        a_block, pair_rows, cot_rows = inputs_now
        new_rows, grad_rows, pulled = pair_update(a_block, factor_b, pair_rows, cot_rows, proj_weight, proj_bias, norm_gain, norm_bias, trans_in, trans_out, S, H)
        grad_a_block = dot_last(factor_b, pulled)
        running = running + jnp.dot(a_block, pulled, preferred_element_type=jnp.float32)
        return (running, (new_rows, grad_rows, grad_a_block))
    start_sum = jnp.zeros((S, R * H), jnp.float32)
    grad_b, outputs = lax.scan(advance, start_sum, (a_blocks, pair_blocks, cot_blocks))
    new_stack, grad_stack, part_stack = outputs
    new_pair = new_stack.reshape(R, R, C)
    pair_grad = grad_stack.reshape(R, R, C)
    grad_a = part_stack.transpose(1, 0, 2).reshape(S, R * H)
    return (new_pair, pair_grad, grad_a, grad_b)
```

```python
import functools
import jax
import jax.numpy as jnp
from jax import lax
from jax.experimental import pallas as pl
from jax.experimental.pallas import tpu as pltpu
from jax.sharding import PartitionSpec as P

F32, BF16 = jnp.float32, jnp.bfloat16


def dot(x, y):
    return jnp.dot(x, y, preferred_element_type=F32)


def turned(x):
    return x.astype(F32).T.astype(BF16)


def prepare_weights(proj_weight, trans_in, trans_out, wide, w_bd, w_bdt, wi, wit, wot):
    wide[0:1024, :] = proj_weight[...].astype(F32) * (1.0 / 128)
    w_bd[...] = jnp.zeros(w_bd.shape, BF16)
    for q in range(16):
        for p in range(2):
            piece = wide[pl.ds(p * 16 + q, 32, stride=32), :].astype(BF16)
            for k in range(2):
                w_bd[q * 128 + p * 64 + k * 32 : q * 128 + p * 64 + k * 32 + 32, k * 128 : k * 128 + 128] = piece
    for q in range(16):
        w_bdt[:, q * 128 : q * 128 + 128] = turned(w_bd[q * 128 : q * 128 + 128, :])
    wi[:, 0:512] = (trans_in[:, 0:512].astype(F32) * 0.5).astype(BF16)
    wi[:, 512:1024] = trans_in[:, 512:1024]
    for q in range(8):
        wit[q * 128 : q * 128 + 128, :] = turned(wi[:, q * 128 : q * 128 + 128])
    for q in range(4):
        wot[:, q * 128 : q * 128 + 128] = turned(trans_out[q * 128 : q * 128 + 128, :])


def prepare_b(b_parts, wide, b_l, b_lt):
    for q in range(16):
        chunk = b_parts[:, :, q * 128 : q * 128 + 128].astype(F32).reshape(128, 128)
        wide[q * 128 : q * 128 + 128, :] = chunk.T
    for q in range(16):
        for p in range(2):
            piece = wide[pl.ds(p * 16 + q, 64, stride=32), :]
            b_l[q * 64 : q * 64 + 64, p * 128 : p * 128 + 128] = piece.astype(BF16)
    for q in range(8):
        b_lt[:, q * 128 : q * 128 + 128] = turned(b_l[q * 128 : q * 128 + 128, :])


def prepare_a(a_parts, a_bd, a_bdt, q):
    chunk = a_parts[:, :, q * 128 : q * 128 + 128].astype(F32).reshape(128, 128)
    other = pltpu.roll(chunk, 64, 1)
    low = lax.broadcasted_iota(jnp.int32, (128, 128), 1) < 64
    zero = jnp.zeros((128, 128), F32)
    at = q * 256
    a_bd[0:128, at : at + 128] = jnp.where(low, chunk, zero).astype(BF16)
    a_bd[128:256, at : at + 128] = jnp.where(low, zero, other).astype(BF16)
    a_bd[0:128, at + 128 : at + 256] = jnp.where(low, other, zero).astype(BF16)
    a_bd[128:256, at + 128 : at + 256] = jnp.where(low, zero, chunk).astype(BF16)
    across = chunk.T.astype(BF16)
    half = jnp.zeros((64, 128), BF16)
    for k in range(2):
        rows = across[k * 64 : k * 64 + 64, :]
        a_bdt[at + k * 128 : at + k * 128 + 64, 0:128] = rows
        a_bdt[at + k * 128 : at + k * 128 + 64, 128:256] = half
        a_bdt[at + k * 128 + 64 : at + k * 128 + 128, 0:128] = half
        a_bdt[at + k * 128 + 64 : at + k * 128 + 128, 128:256] = rows


def fold(y, n):
    out = []
    low = lax.broadcasted_iota(jnp.int32, (128, 128), 1) < 64
    for m in range(0, n, 2):
        e0 = y[0:128, m * 128 : m * 128 + 128]
        e1 = y[128:256, m * 128 : m * 128 + 128]
        o0 = y[0:128, m * 128 + 128 : m * 128 + 256]
        o1 = y[128:256, m * 128 + 128 : m * 128 + 256]
        out.append(jnp.where(low, e0, o1) + pltpu.roll(jnp.where(low, o0, e1), 64, 1))
    return out


def pair_block(ib, nb, pair, cot, bias, gain, shift, wi, wit, wo, wot, b_l, b_lt, a_bd, a_bdt, w_bd, w_bdt, xs, ps, new_pair, pair_grad):
    at = pl.multiple_of(ib * (nb * 128), nb * 128)
    rows = nb * 128
    for t in range(nb // 2):
        x = dot(b_l[...], a_bd[:, pl.ds(at + t * 256, 256)]).astype(BF16)
        for q in range(16):
            for k in range(2):
                xs[(2 * t + k) * 64 : (2 * t + k) * 64 + 64, q * 128 : q * 128 + 128] = x[q * 64 : q * 64 + 64, k * 128 : k * 128 + 128]
    proj = dot(xs[...], w_bd[...])
    proj = jnp.concatenate([proj[(k // 2) * 64 : (k // 2) * 64 + 64, (k % 2) * 128 : (k % 2) * 128 + 128] for k in range(2 * nb)], axis=0)
    first = pl.multiple_of(ib * rows, rows)
    updated = pair[pl.ds(first, rows), :].astype(F32) + (proj + bias[...])
    mu = jnp.mean(updated, axis=-1, keepdims=True)
    centered = updated - mu
    var = jnp.mean(centered * centered, axis=-1, keepdims=True)
    inv = lax.rsqrt(var + 1e-05)
    normed = centered * inv
    ln = (normed * gain[...] + shift[...]).astype(BF16)
    cot_here = cot[pl.ds(first, rows), :]
    both = dot(ln, wi[...])
    dh = dot(cot_here, wot[...])
    half = both[:, 0:512]
    up = both[:, 512:1024]
    q = 1.0 + jnp.tanh(half)
    act = half * q
    hidden = (act * up).astype(BF16)
    new_pair[pl.ds(first, rows), :] = (updated + dot(hidden, wo[...])).astype(BF16)
    d_up = (dh * act).astype(BF16)
    d_gate = (dh * up * (q + act * (2.0 - q))).astype(BF16)
    dn = (dot(d_gate, wit[0:512, :]) + dot(d_up, wit[512:1024, :])) * gain[...]
    m1 = jnp.mean(dn, axis=-1, keepdims=True)
    m2 = jnp.mean(dn * normed, axis=-1, keepdims=True)
    g = (cot_here.astype(F32) + inv * (dn - m1 - normed * m2)).astype(BF16)
    pair_grad[pl.ds(first, rows), :] = g
    g2 = jnp.concatenate(
        [jnp.concatenate([g[(2 * k) * 64 : (2 * k) * 64 + 64], g[(2 * k + 1) * 64 : (2 * k + 1) * 64 + 64]], axis=1) for k in range(nb)], axis=0
    )
    for t in range(8):
        pulled = dot(g2, w_bdt[:, t * 256 : t * 256 + 256]).astype(BF16)
        for k in range(nb):
            for m in range(2):
                q = 2 * t + m
                ps[q * 64 : q * 64 + 64, k * 128 : k * 128 + 128] = pulled[k * 64 : k * 64 + 64, m * 128 : m * 128 + 128]


MESH = pl.DeviceIdType.MESH
NB = 16
PEERS = 16


def here():
    return lax.axis_index("row"), lax.axis_index("col")


def greet(devices, count):
    barrier = pltpu.get_barrier_semaphore()
    for ok, where in devices:
        if ok is None:
            pl.semaphore_signal(barrier, inc=1, device_id=where, device_id_type=MESH)
        else:

            @pl.when(ok)
            def _(where=where):
                pl.semaphore_signal(barrier, inc=1, device_id=where, device_id_type=MESH)

    pl.semaphore_wait(barrier, count)


def gather_kernel(a, b, a_parts, b_parts, a_send, a_recv, b_send, b_recv):
    r, c = here()
    diagonal = r == c
    greetings = [(None, ((r + k) % PEERS, c)) for k in range(1, PEERS)]
    greetings += [(((r + k) % PEERS != r) | (c != r), ((r + k) % PEERS, r)) for k in range(PEERS)]
    greet(greetings, 2 * PEERS - 1 - diagonal.astype(jnp.int32))

    def b_copy(k):
        return pltpu.make_async_remote_copy(
            src_ref=b, dst_ref=b_parts.at[r], send_sem=b_send.at[k], recv_sem=b_recv.at[r],
            device_id=((r + k) % PEERS, c), device_id_type=MESH)

    def a_copy(k):
        return pltpu.make_async_remote_copy(
            src_ref=a, dst_ref=a_parts.at[r], send_sem=a_send.at[k], recv_sem=a_recv.at[r],
            device_id=(c, (c + k) % PEERS), device_id_type=MESH)

    own_b = pltpu.make_async_copy(b, b_parts.at[r], b_recv.at[r])
    own_b.start()
    own_a = pltpu.make_async_copy(a, a_parts.at[r], a_recv.at[r])

    @pl.when(diagonal)
    def _():
        own_a.start()

    @pl.when(jnp.logical_not(diagonal))
    def _():
        a_copy(0).start()

    for k in range(1, PEERS):
        a_copy(k).start()
        b_copy(k).start()

    for k in range(PEERS):
        pltpu.make_async_copy(b, b_parts.at[k], b_recv.at[k]).wait()
        pltpu.make_async_copy(a, a_parts.at[k], a_recv.at[k]).wait()
    for k in range(1, PEERS):
        a_copy(k).wait_send()
        b_copy(k).wait_send()

    @pl.when(jnp.logical_not(diagonal))
    def _():
        a_copy(0).wait_send()


def gather(a, b):
    vm = pl.BlockSpec(memory_space=pltpu.VMEM)
    return pl.pallas_call(
        gather_kernel,
        out_shape=(jax.ShapeDtypeStruct((PEERS, *a.shape), BF16),) * 2,
        in_specs=[vm] * 2,
        out_specs=(vm,) * 2,
        scratch_shapes=[pltpu.SemaphoreType.DMA((PEERS,))] * 4,
        compiler_params=pltpu.CompilerParams(collective_id=0, has_side_effects=True),
        name="gather",
    )(a, b)


def scatter_kernel(ga, gb, grad_a, grad_b, a_in, b_in, wide, a_send, a_recv, b_send, b_recv):
    r, c = here()
    diagonal = r == c
    greetings = [(None, ((r + k) % PEERS, c)) for k in range(1, PEERS)]
    greetings += [(((c + k) % PEERS != c) | (c != r), (c, (c + k) % PEERS)) for k in range(PEERS)]
    greet(greetings, 2 * PEERS - 1 - diagonal.astype(jnp.int32))

    def a_copy(k):
        to = (r + k) % PEERS
        return pltpu.make_async_remote_copy(
            src_ref=ga.at[to], dst_ref=a_in.at[c], send_sem=a_send.at[k], recv_sem=a_recv.at[c],
            device_id=(to, r), device_id_type=MESH)

    def b_copy(k):
        to = (r + k) % PEERS
        return pltpu.make_async_remote_copy(
            src_ref=gb.at[to], dst_ref=b_in.at[r], send_sem=b_send.at[k], recv_sem=b_recv.at[r],
            device_id=(to, c), device_id_type=MESH)

    pltpu.make_async_copy(gb.at[r], b_in.at[r], b_recv.at[r]).start()

    @pl.when(diagonal)
    def _():
        pltpu.make_async_copy(ga.at[r], a_in.at[c], a_recv.at[c]).start()

    @pl.when(jnp.logical_not(diagonal))
    def _():
        a_copy(0).start()

    for k in range(1, PEERS):
        a_copy(k).start()
        b_copy(k).start()

    for k in range(PEERS):
        pltpu.make_async_copy(gb.at[k], b_in.at[k], b_recv.at[k]).wait()
        pltpu.make_async_copy(ga.at[k], a_in.at[k], a_recv.at[k]).wait()
    for k in range(1, PEERS):
        a_copy(k).wait_send()
        b_copy(k).wait_send()

    @pl.when(jnp.logical_not(diagonal))
    def _():
        a_copy(0).wait_send()

    finish_a(a_in, grad_a)
    finish_b(b_in, wide, grad_b)


def finish_a(a_in, grad_a):
    for t in range(8):
        total = jnp.sum(a_in[:, :, t * 128 : t * 128 + 128].astype(F32), axis=0)
        blk, sub = t // 4, t % 4
        for k in range(2):
            at = blk * 1024 + k * 512 + sub * 128
            grad_a[:, at : at + 128] = total[k * 8 : k * 8 + 8]


def finish_b(b_in, wide, grad_b):
    for t in range(8):
        total = jnp.sum(b_in[:, :, t * 128 : t * 128 + 128].astype(F32), axis=0)
        across = jnp.concatenate([total, jnp.zeros((112, 128), F32)], axis=0).T
        for k in range(2):
            q = 2 * t + k
            rows = across[k * 64 : k * 64 + 64]
            wide[pl.ds(q, 64, stride=32), :] = rows
            wide[pl.ds(16 + q, 64, stride=32), :] = pltpu.roll(rows, 120, 1)
    for t in range(16):
        grad_b[:, t * 128 : t * 128 + 128] = wide[t * 128 : t * 128 + 128, :].T[0:8]


def scatter(ga, gb):
    vm = pl.BlockSpec(memory_space=pltpu.VMEM)
    return pl.pallas_call(
        scatter_kernel,
        out_shape=(jax.ShapeDtypeStruct((8, 2048), F32),) * 2,
        in_specs=[vm] * 2,
        out_specs=(vm,) * 2,
        scratch_shapes=[
            pltpu.VMEM((PEERS, 16, 1024), BF16),
            pltpu.VMEM((PEERS, 16, 1024), BF16),
            pltpu.VMEM((2048, 128), F32),
        ]
        + [pltpu.SemaphoreType.DMA((PEERS,))] * 4,
        compiler_params=pltpu.CompilerParams(collective_id=1, has_side_effects=True),
        name="scatter",
    )(ga, gb)


def tile_kernel(nb, a_parts, b_parts, pair, cot, proj_weight, bias, gain, shift, trans_in, trans_out, new_pair, pair_grad, ga, gb,
                wide, w_bd, w_bdt, wi, wit, wot, b_l, b_lt, a_bd, a_bdt, xs, ps, acc):
    prepare_weights(proj_weight, trans_in, trans_out, wide, w_bd, w_bdt, wi, wit, wot)
    prepare_b(b_parts, wide, b_l, b_lt)
    for q in range(16):
        prepare_a(a_parts, a_bd, a_bdt, q)
    acc[...] = jnp.zeros(acc.shape, F32)

    def step(ib, _):
        pair_block(ib, nb, pair, cot, bias, gain, shift, wi, wit, trans_out, wot, b_l, b_lt, a_bd, a_bdt, w_bd, w_bdt, xs, ps, new_pair, pair_grad)
        pieces = fold(dot(b_lt[...], ps[...]), nb)
        at = pl.multiple_of(ib * (nb * 32), nb * 32)
        for m in range(nb // 4):
            two = [pieces[m + k * (nb // 4)].reshape(PEERS, 8, 128) for k in range(2)]
            ga[:, :, pl.ds(at + m * 128, 128)] = jnp.concatenate(two, axis=1).astype(BF16)
        start = pl.multiple_of(ib * (nb * 128), nb * 128)
        acc[...] += dot(ps[...], a_bdt[pl.ds(start, nb * 128), :])
        return 0

    lax.fori_loop(0, 32 // nb, step, 0)
    for q in range(8):
        across = acc[q * 128 : q * 128 + 128, :].T
        two = [across[p * 128 : p * 128 + 128].reshape(PEERS, 8, 128) for p in range(2)]
        gb[:, :, q * 128 : q * 128 + 128] = jnp.concatenate(two, axis=1).astype(BF16)


def tile_call(nb, a_parts, b_parts, pair, cot, proj_weight, bias, gain, shift, trans_in, trans_out):
    S = jax.ShapeDtypeStruct
    vm = pl.BlockSpec(memory_space=pltpu.VMEM)
    return pl.pallas_call(
        functools.partial(tile_kernel, nb),
        out_shape=(S((4096, 128), BF16), S((4096, 128), BF16), S((16, 16, 1024), BF16), S((16, 16, 1024), BF16)),
        in_specs=[vm] * 10,
        out_specs=(vm,) * 4,
        scratch_shapes=[
            pltpu.VMEM((2048, 128), F32),
            pltpu.VMEM((2048, 256), BF16),
            pltpu.VMEM((256, 2048), BF16),
            pltpu.VMEM((128, 1024), BF16),
            pltpu.VMEM((1024, 128), BF16),
            pltpu.VMEM((128, 512), BF16),
            pltpu.VMEM((1024, 256), BF16),
            pltpu.VMEM((256, 1024), BF16),
            pltpu.VMEM((256, 4096), BF16),
            pltpu.VMEM((4096, 256), BF16),
            pltpu.VMEM((nb * 64, 2048), BF16),
            pltpu.VMEM((1024, nb * 128), BF16),
            pltpu.VMEM((1024, 256), F32),
        ],
        compiler_params=pltpu.CompilerParams(vmem_limit_bytes=58 << 20),
        name="tile",
    )(a_parts, b_parts, pair, cot, proj_weight, bias, gain, shift, trans_in, trans_out)


def body(factor_a, factor_b, pair, proj_weight, proj_bias, norm_gain, norm_bias, trans_in, trans_out, cotangent):
    a_parts, b_parts = gather(factor_a, factor_b)
    new_pair, pair_grad, ga, gb = tile_call(
        NB, a_parts, b_parts, pair.reshape(4096, 128), cotangent.reshape(4096, 128), proj_weight,
        proj_bias.reshape(1, 128), norm_gain.reshape(1, 128), norm_bias.reshape(1, 128), trans_in, trans_out)
    grad_a, grad_b = scatter(ga, gb)
    return new_pair.reshape(pair.shape), pair_grad.reshape(pair.shape), grad_a, grad_b


def solution(mesh):
    tiles = P("row", "col", None)
    return jax.shard_map(
        body,
        mesh=mesh,
        in_specs=(P("row", "col"), P("row", "col"), tiles, P(), P(), P(), P(), P(), P(), tiles),
        out_specs=(tiles, tiles, P("row", "col"), P("row", "col")),
        check_vma=False,
    )
```

```python
import functools
import jax
import jax.numpy as jnp
from jax import lax
from jax.experimental import pallas as pl
from jax.experimental.pallas import tpu as pltpu
from jax.sharding import PartitionSpec as P

F32, BF16 = jnp.float32, jnp.bfloat16


def dot(x, y):
    return jnp.dot(x, y, preferred_element_type=F32)


def turned(x):
    return x.astype(F32).T.astype(BF16)


def prepare_weights(proj_weight, trans_in, trans_out, wide, w_bd, w_bdt, wi, wit, wot):
    wide[0:1024, :] = proj_weight[...].astype(F32) * (1.0 / 128)
    w_bd[...] = jnp.zeros(w_bd.shape, BF16)
    for q in range(16):
        for p in range(2):
            piece = wide[pl.ds(p * 16 + q, 32, stride=32), :].astype(BF16)
            for k in range(2):
                w_bd[q * 128 + p * 64 + k * 32 : q * 128 + p * 64 + k * 32 + 32, k * 128 : k * 128 + 128] = piece
    for q in range(16):
        w_bdt[:, q * 128 : q * 128 + 128] = turned(w_bd[q * 128 : q * 128 + 128, :])
    wi[:, 0:512] = (trans_in[:, 0:512].astype(F32) * 0.5).astype(BF16)
    wi[:, 512:1024] = trans_in[:, 512:1024]
    for q in range(8):
        wit[q * 128 : q * 128 + 128, :] = turned(wi[:, q * 128 : q * 128 + 128])
    for q in range(4):
        wot[:, q * 128 : q * 128 + 128] = turned(trans_out[q * 128 : q * 128 + 128, :])


def prepare_b(b_parts, wide, b_l, b_lt):
    for q in range(16):
        chunk = b_parts[:, :, q * 128 : q * 128 + 128].astype(F32).reshape(128, 128)
        wide[q * 128 : q * 128 + 128, :] = chunk.T
    for q in range(16):
        for p in range(2):
            piece = wide[pl.ds(p * 16 + q, 64, stride=32), :]
            b_l[q * 64 : q * 64 + 64, p * 128 : p * 128 + 128] = piece.astype(BF16)
    for q in range(8):
        b_lt[:, q * 128 : q * 128 + 128] = turned(b_l[q * 128 : q * 128 + 128, :])


def prepare_a(a_parts, a_bd, at):
    chunk = a_parts.astype(F32).reshape(128, 128)
    other = pltpu.roll(chunk, 64, 1)
    low = lax.broadcasted_iota(jnp.int32, (128, 128), 1) < 64
    zero = jnp.zeros((128, 128), F32)
    a_bd[0:128, pl.ds(at, 128)] = jnp.where(low, chunk, zero).astype(BF16)
    a_bd[128:256, pl.ds(at, 128)] = jnp.where(low, zero, other).astype(BF16)
    a_bd[0:128, pl.ds(at + 128, 128)] = jnp.where(low, other, zero).astype(BF16)
    a_bd[128:256, pl.ds(at + 128, 128)] = jnp.where(low, zero, chunk).astype(BF16)


def fold(y, n):
    out = []
    low = lax.broadcasted_iota(jnp.int32, (128, 128), 1) < 64
    for m in range(0, n, 2):
        e0 = y[0:128, m * 128 : m * 128 + 128]
        e1 = y[128:256, m * 128 : m * 128 + 128]
        o0 = y[0:128, m * 128 + 128 : m * 128 + 256]
        o1 = y[128:256, m * 128 + 128 : m * 128 + 256]
        out.append(jnp.where(low, e0, o1) + pltpu.roll(jnp.where(low, o0, e1), 64, 1))
    return out


MESH = pl.DeviceIdType.MESH
NB = 8
BLOCKS = 32 // NB
PEERS = 16


def dot_last(x, y):
    return lax.dot_general(x, y, (((1,), (1,)), ((), ())), preferred_element_type=F32)


def pair_block(ib, pair, cot, bias, gain, shift, wi, wit, wo, wot, b_l, a_bd, w_bd, w_bdt, xs, ps, new_pair, pair_grad):
    nb = NB
    rows = nb * 128
    at = pl.multiple_of(ib * rows, rows)
    x = dot(b_l[...], a_bd[:, pl.ds(at, rows)]).astype(BF16)
    for q in range(16):
        for k in range(nb):
            xs[k * 64 : k * 64 + 64, q * 128 : q * 128 + 128] = x[q * 64 : q * 64 + 64, k * 128 : k * 128 + 128]
    proj = dot(xs[...], w_bd[...])
    proj = jnp.concatenate(
        [proj[(k // 2) * 64 : (k // 2) * 64 + 64, (k % 2) * 128 : (k % 2) * 128 + 128] for k in range(2 * nb)], axis=0)
    updated = pair[pl.ds(at, rows), :].astype(F32) + (proj + bias[...])
    mu = jnp.mean(updated, axis=-1, keepdims=True)
    centered = updated - mu
    var = jnp.mean(centered * centered, axis=-1, keepdims=True)
    inv = lax.rsqrt(var + 1e-05)
    normed = centered * inv
    ln = (normed * gain[...] + shift[...]).astype(BF16)
    cot_here = cot[pl.ds(at, rows), :]
    both = dot(ln, wi[...])
    dh = dot(cot_here, wot[...])
    half = both[:, 0:512]
    up = both[:, 512:1024]
    q = 1.0 + jnp.tanh(half)
    act = half * q
    hidden = (act * up).astype(BF16)
    new_pair[pl.ds(at, rows), :] = (updated + dot(hidden, wo[...])).astype(BF16)
    d_up = (dh * act).astype(BF16)
    d_gate = (dh * up * (q + act * (2.0 - q))).astype(BF16)
    dn = (dot(d_gate, wit[0:512, :]) + dot(d_up, wit[512:1024, :])) * gain[...]
    m1 = jnp.mean(dn, axis=-1, keepdims=True)
    m2 = jnp.mean(dn * normed, axis=-1, keepdims=True)
    g = (cot_here.astype(F32) + inv * (dn - m1 - normed * m2)).astype(BF16)
    pair_grad[pl.ds(at, rows), :] = g
    g2 = jnp.concatenate(
        [jnp.concatenate([g[2 * k * 64 : 2 * k * 64 + 64], g[2 * k * 64 + 64 : 2 * k * 64 + 128]], axis=1) for k in range(nb)],
        axis=0)
    pulled = dot(g2, w_bdt[...]).astype(BF16)
    for q in range(16):
        for k in range(nb):
            ps[q * 64 : q * 64 + 64, pl.ds(at + k * 128, 128)] = pulled[k * 64 : k * 64 + 64, q * 128 : q * 128 + 128]


def arrived(ref, sem):
    pltpu.make_async_copy(ref, ref, sem).wait()


def kernel(
    a, b, pair_h, cot_h, weight_h, bias, gain, shift, in_h, out_h,
    new_h, pair_grad_h, grad_a, grad_b,
    pair, cot, weight, trans_in, trans_out, new_pair, pair_grad,
    a_parts, b_parts, wide, w_bd, w_bdt, wi, wit, wot, b_l, b_lt, a_bd, xs, ps,
    ga_out, ga_in, ga_sum, ga_back, gb_out, gb_in,
    load_sem, store_sem, a_send, a_recv, a_first, b_send, b_recv,
    g1_send, g1_recv, g2_send, g2_recv, gb_send, gb_recv,
):
    r, c = lax.axis_index("row"), lax.axis_index("col")
    diagonal = r == c
    off = jnp.logical_not(diagonal)
    remote = functools.partial(pltpu.make_async_remote_copy, device_id_type=MESH)

    loads = [
        pltpu.make_async_copy(x, y, load_sem.at[k])
        for k, (x, y) in enumerate(
            [(weight_h, weight), (in_h, trans_in), (out_h, trans_out), (pair_h, pair), (cot_h, cot)])
    ]
    for copy in loads:
        copy.start()

    barrier = pltpu.get_barrier_semaphore()

    def greet(where):
        pl.semaphore_signal(barrier, inc=1, device_id=where, device_id_type=MESH)

    for k in range(1, PEERS):
        greet(((r + k) % PEERS, c))
        greet((((c + k) % PEERS), r))
        greet((r, (c + k) % PEERS))

    @pl.when(off)
    def _():
        greet((c, r))

    for copy in loads[:3]:
        copy.wait()
    prepare_weights(weight, trans_in, trans_out, wide, w_bd, w_bdt, wi, wit, wot)
    pl.semaphore_wait(barrier, 3 * (PEERS - 1) + off.astype(jnp.int32))

    def b_copy(k):
        return remote(
            src_ref=b, dst_ref=b_parts.at[r], send_sem=b_send, recv_sem=b_recv, device_id=((r + k) % PEERS, c))

    def a_copy(k, ib):
        sem = a_first.at[ib] if k == 0 else a_send.at[ib]
        return remote(
            src_ref=a.at[:, pl.ds(pl.multiple_of(ib * (NB * 64), NB * 64), NB * 64)], dst_ref=a_parts.at[ib, r],
            send_sem=sem, recv_sem=a_recv.at[ib], device_id=(c, (r + k) % PEERS))

    pltpu.make_async_copy(b, b_parts.at[r], b_recv).start()
    for k in range(1, PEERS):
        b_copy(k).start()

    def give_a(ib, _):
        @pl.when(diagonal)
        def _():
            pltpu.make_async_copy(
                a.at[:, pl.ds(pl.multiple_of(ib * (NB * 64), NB * 64), NB * 64)], a_parts.at[ib, r], a_recv.at[ib]).start()

        @pl.when(off)
        def _():
            a_copy(0, ib).start()

        for k in range(1, PEERS):
            a_copy(k, ib).start()
        return 0

    lax.fori_loop(0, BLOCKS, give_a, 0)

    for copy in loads[3:]:
        copy.wait()
    arrived(b_parts, b_recv)
    prepare_b(b_parts, wide, b_l, b_lt)

    def g1_copy(k, ib):
        to = (c + k) % PEERS
        return remote(
            src_ref=ga_out.at[ib, to], dst_ref=ga_in.at[ib, c], send_sem=g1_send.at[ib], recv_sem=g1_recv.at[ib],
            device_id=(r, to))

    def g2_copy(ib):
        return remote(
            src_ref=ga_sum.at[ib], dst_ref=ga_back.at[ib], send_sem=g2_send.at[ib], recv_sem=g2_recv.at[ib], device_id=(c, r))

    def combine(ib):
        arrived(ga_in.at[ib], g1_recv.at[ib])
        for m in range(NB // 4):
            ga_sum[ib, :, m * 128 : m * 128 + 128] = jnp.sum(ga_in[ib, :, :, m * 128 : m * 128 + 128].astype(F32), axis=0)

        @pl.when(diagonal)
        def _():
            pltpu.make_async_copy(ga_sum.at[ib], ga_back.at[ib], g2_recv.at[ib]).start()

        @pl.when(off)
        def _():
            g2_copy(ib).start()

    def store(x, y, ib, k):
        part = pl.ds(pl.multiple_of(ib * (NB * 128), NB * 128), NB * 128)
        return pltpu.make_async_copy(x.at[part], y.at[part], store_sem.at[k, ib])

    def step(ib, _):
        arrived(a_parts.at[ib], a_recv.at[ib])
        at = pl.multiple_of(ib * (NB * 128), NB * 128)
        for k in range(NB // 2):
            prepare_a(a_parts[ib, :, :, k * 128 : k * 128 + 128], a_bd, at + k * 256)
        pair_block(ib, pair, cot, bias, gain, shift, wi, wit, trans_out, wot, b_l, a_bd, w_bd, w_bdt, xs, ps, new_pair, pair_grad)
        store(new_pair, new_h, ib, 0).start()
        store(pair_grad, pair_grad_h, ib, 1).start()
        pieces = fold(dot(b_lt[...], ps[:, pl.ds(at, NB * 128)]), NB)
        for m in range(NB // 4):
            two = [pieces[m + k * (NB // 4)].reshape(PEERS, 8, 128) for k in range(2)]
            ga_out[ib, :, :, m * 128 : m * 128 + 128] = jnp.concatenate(two, axis=1).astype(BF16)
        pltpu.make_async_copy(ga_out.at[ib, c], ga_in.at[ib, c], g1_recv.at[ib]).start()
        for k in range(1, PEERS):
            g1_copy(k, ib).start()

        @pl.when(ib >= 2)
        def _():
            combine(ib - 2)

        return 0

    lax.fori_loop(0, BLOCKS, step, 0)

    def gb_copy(k, h):
        to = (r + k) % PEERS
        return remote(
            src_ref=gb_out.at[h, to], dst_ref=gb_in.at[h, r], send_sem=gb_send.at[h], recv_sem=gb_recv.at[h],
            device_id=(to, c))

    for h in range(2):
        g = dot_last(a_bd[...], ps[h * 512 : h * 512 + 512, :])
        two = [g[p * 128 : p * 128 + 128].reshape(PEERS, 8, 512) for p in range(2)]
        gb_out[h] = jnp.concatenate(two, axis=1).astype(BF16)
        pltpu.make_async_copy(gb_out.at[h, r], gb_in.at[h, r], gb_recv.at[h]).start()
        for k in range(1, PEERS):
            gb_copy(k, h).start()
    combine(BLOCKS - 2)
    combine(BLOCKS - 1)

    for h in range(2):
        arrived(gb_in.at[h], gb_recv.at[h])
        for t in range(4):
            total = jnp.sum(gb_in[h, :, :, t * 128 : t * 128 + 128].astype(F32), axis=0)
            across = jnp.concatenate([total, jnp.zeros((112, 128), F32)], axis=0).T
            for k in range(2):
                q = 8 * h + 2 * t + k
                rows = across[k * 64 : k * 64 + 64]
                wide[pl.ds(q, 64, stride=32), :] = rows
                wide[pl.ds(16 + q, 64, stride=32), :] = pltpu.roll(rows, 120, 1)
    for t in range(16):
        grad_b[:, t * 128 : t * 128 + 128] = wide[t * 128 : t * 128 + 128, :].T[0:8]

    for ib in range(BLOCKS):
        arrived(ga_back.at[ib], g2_recv.at[ib])
        for k in range(2):
            at = ib * (NB * 64) + k * (NB * 32)
            grad_a[:, at : at + NB * 32] = ga_back[ib, k * 8 : k * 8 + 8, :]

    arrived(b_parts.at[0 : PEERS - 1], b_send)
    for h in range(2):
        arrived(gb_out.at[h, 0 : PEERS - 1], gb_send.at[h])
    for ib in range(BLOCKS):
        arrived(a_parts.at[ib, 0 : PEERS - 1], a_send.at[ib])
        arrived(ga_out.at[ib, 0 : PEERS - 1], g1_send.at[ib])
        store(new_pair, new_h, ib, 0).wait()
        store(pair_grad, pair_grad_h, ib, 1).wait()

        @pl.when(off)
        def _(ib=ib):
            a_copy(0, ib).wait_send()
            g2_copy(ib).wait_send()


def body(factor_a, factor_b, pair, proj_weight, proj_bias, norm_gain, norm_bias, trans_in, trans_out, cotangent):
    S = jax.ShapeDtypeStruct
    vmem = pl.BlockSpec(memory_space=pltpu.VMEM)
    hbm = pl.BlockSpec(memory_space=pl.ANY)
    V = pltpu.VMEM
    D = pltpu.SemaphoreType.DMA
    new_pair, pair_grad, grad_a, grad_b = pl.pallas_call(
        kernel,
        out_shape=(S((4096, 128), BF16), S((4096, 128), BF16), S((8, 2048), F32), S((8, 2048), F32)),
        in_specs=[vmem, vmem, hbm, hbm, hbm, vmem, vmem, vmem, hbm, hbm],
        out_specs=(hbm, hbm, vmem, vmem),
        scratch_shapes=[
            V((4096, 128), BF16), V((4096, 128), BF16), V((1024, 128), BF16), V((128, 1024), BF16), V((512, 128), BF16),
            V((4096, 128), BF16), V((4096, 128), BF16),
            V((BLOCKS, PEERS, 8, NB * 64), BF16), V((PEERS, 8, 2048), BF16),
            V((2048, 128), F32), V((2048, 256), BF16), V((256, 2048), BF16),
            V((128, 1024), BF16), V((1024, 128), BF16), V((128, 512), BF16),
            V((1024, 256), BF16), V((256, 1024), BF16), V((256, 4096), BF16),
            V((NB * 64, 2048), BF16), V((1024, 4096), BF16),
            V((BLOCKS, PEERS, 16, NB * 32), BF16), V((BLOCKS, PEERS, 16, NB * 32), BF16),
            V((BLOCKS, 16, NB * 32), F32), V((BLOCKS, 16, NB * 32), F32),
            V((2, PEERS, 16, 512), BF16), V((2, PEERS, 16, 512), BF16),
            D((5,)), D((2, BLOCKS)), D((BLOCKS,)), D((BLOCKS,)), D((BLOCKS,)), D, D,
            D((BLOCKS,)), D((BLOCKS,)), D((BLOCKS,)), D((BLOCKS,)), D((2,)), D((2,)),
        ],
        compiler_params=pltpu.CompilerParams(collective_id=0, has_side_effects=True, vmem_limit_bytes=58 << 20),
        name="whole",
    )(
        factor_a, factor_b, pair.reshape(4096, 128), cotangent.reshape(4096, 128), proj_weight,
        proj_bias.reshape(1, 128), norm_gain.reshape(1, 128), norm_bias.reshape(1, 128), trans_in, trans_out)
    return new_pair.reshape(pair.shape), pair_grad.reshape(pair.shape), grad_a, grad_b


def solution(mesh):
    tiles = P("row", "col", None)
    return jax.shard_map(
        body,
        mesh=mesh,
        in_specs=(P("row", "col"), P("row", "col"), tiles, P(), P(), P(), P(), P(), P(), tiles),
        out_specs=(tiles, tiles, P("row", "col"), P("row", "col")),
        check_vma=False,
    )
```

```python
import functools
import jax
import jax.numpy as jnp
from jax import lax
from jax.experimental import pallas as pl
from jax.experimental.pallas import tpu as pltpu
from jax.sharding import PartitionSpec as P

F32, BF16 = jnp.float32, jnp.bfloat16


def dot(x, y):
    return jnp.dot(x, y, preferred_element_type=F32)


def turned(x):
    return x.astype(F32).T.astype(BF16)


def prepare_weights(proj_weight, trans_in, trans_out, wide, w_bd, w_bdt, wi, wit, wot):
    wide[0:1024, :] = proj_weight[...].astype(F32) * (1.0 / 128)
    w_bd[...] = jnp.zeros(w_bd.shape, BF16)
    for q in range(16):
        for p in range(2):
            piece = wide[pl.ds(p * 16 + q, 32, stride=32), :].astype(BF16)
            for k in range(2):
                w_bd[q * 128 + p * 64 + k * 32 : q * 128 + p * 64 + k * 32 + 32, k * 128 : k * 128 + 128] = piece
    for q in range(16):
        w_bdt[:, q * 128 : q * 128 + 128] = turned(w_bd[q * 128 : q * 128 + 128, :])
    wi[:, 0:512] = (trans_in[:, 0:512].astype(F32) * 0.5).astype(BF16)
    wi[:, 512:1024] = trans_in[:, 512:1024]
    for q in range(8):
        wit[q * 128 : q * 128 + 128, :] = turned(wi[:, q * 128 : q * 128 + 128])
    for q in range(4):
        wot[:, q * 128 : q * 128 + 128] = turned(trans_out[q * 128 : q * 128 + 128, :])


def prepare_b(b_parts, wide, b_l, b_lt):
    for q in range(16):
        chunk = b_parts[:, :, q * 128 : q * 128 + 128].astype(F32).reshape(128, 128)
        wide[q * 128 : q * 128 + 128, :] = chunk.T
    for q in range(16):
        for p in range(2):
            piece = wide[pl.ds(p * 16 + q, 64, stride=32), :]
            b_l[q * 64 : q * 64 + 64, p * 128 : p * 128 + 128] = piece.astype(BF16)
    for q in range(8):
        b_lt[:, q * 128 : q * 128 + 128] = turned(b_l[q * 128 : q * 128 + 128, :])


def prepare_a(a_parts, a_bd, at):
    chunk = a_parts.astype(F32).reshape(128, 128)
    other = pltpu.roll(chunk, 64, 1)
    low = lax.broadcasted_iota(jnp.int32, (128, 128), 1) < 64
    zero = jnp.zeros((128, 128), F32)
    a_bd[0:128, pl.ds(at, 128)] = jnp.where(low, chunk, zero).astype(BF16)
    a_bd[128:256, pl.ds(at, 128)] = jnp.where(low, zero, other).astype(BF16)
    a_bd[0:128, pl.ds(at + 128, 128)] = jnp.where(low, other, zero).astype(BF16)
    a_bd[128:256, pl.ds(at + 128, 128)] = jnp.where(low, zero, chunk).astype(BF16)


def fold(y, n):
    out = []
    low = lax.broadcasted_iota(jnp.int32, (128, 128), 1) < 64
    for m in range(0, n, 2):
        e0 = y[0:128, m * 128 : m * 128 + 128]
        e1 = y[128:256, m * 128 : m * 128 + 128]
        o0 = y[0:128, m * 128 + 128 : m * 128 + 256]
        o1 = y[128:256, m * 128 + 128 : m * 128 + 256]
        out.append(jnp.where(low, e0, o1) + pltpu.roll(jnp.where(low, o0, e1), 64, 1))
    return out


MESH = pl.DeviceIdType.MESH
NB = 8
BLOCKS = 32 // NB
ROWS = NB * 128
CHUNK = 256
PEERS = 16


def dot_last(x, y):
    return lax.dot_general(x, y, (((1,), (1,)), ((), ())), preferred_element_type=F32)


def projected(ib, b_l, a_bd, w_bd, proj):
    at = pl.multiple_of(ib * ROWS, ROWS)
    for c in range(4):
        x = dot(b_l[c * 256 : c * 256 + 256, :], a_bd[:, pl.ds(at, ROWS)]).astype(BF16)
        x = jnp.concatenate(
            [
                jnp.concatenate([x[q * 64 : q * 64 + 64, k * 128 : k * 128 + 128] for q in range(4)], axis=1)
                for k in range(NB)
            ],
            axis=0)
        part = dot(x, w_bd[c * 512 : c * 512 + 512, :])
        if c == 0:
            proj[...] = part
        else:
            proj[...] += part


def pair_rows(at, first, pair, cot, proj, bias, gain, shift, wi, wit, wot, updated_all, hidden_all, pair_grad):
    here = pl.ds(at, CHUNK)
    parts = [
        proj[(k // 2) * 64 : (k // 2) * 64 + 64, (k % 2) * 128 : (k % 2) * 128 + 128]
        for k in range(first // 64, (first + CHUNK) // 64)
    ]
    updated = pair[here, :].astype(F32) + (jnp.concatenate(parts, axis=0) + bias[...])
    updated_all[here, :] = updated
    mu = jnp.mean(updated, axis=-1, keepdims=True)
    centered = updated - mu
    var = jnp.mean(centered * centered, axis=-1, keepdims=True)
    inv = lax.rsqrt(var + 1e-05)
    normed = centered * inv
    ln = (normed * gain[...] + shift[...]).astype(BF16)
    cot_here = cot[here, :]
    half = dot(ln, wi[:, 0:512])
    up = dot(ln, wi[:, 512:1024])
    dh = dot(cot_here, wot[...])
    q = 1.0 + jnp.tanh(half)
    act = half * q
    hidden_all[here, :] = (act * up).astype(BF16)
    d_up = (dh * act).astype(BF16)
    d_gate = (dh * up * (q + act * (2.0 - q))).astype(BF16)
    dn = dot(jnp.concatenate([d_gate, d_up], axis=1), wit[...]) * gain[...]
    m1 = jnp.mean(dn, axis=-1, keepdims=True)
    m2 = jnp.mean(dn * normed, axis=-1, keepdims=True)
    g = (cot_here.astype(F32) + inv * (dn - m1 - normed * m2)).astype(BF16)
    pair_grad[here, :] = g
    return [
        jnp.concatenate([g[k * 128 : k * 128 + 64], g[k * 128 + 64 : k * 128 + 128]], axis=1) for k in range(CHUNK // 128)
    ]


def pair_block(ib, pair, cot, bias, gain, shift, wi, wit, wot, b_l, a_bd, w_bd, w_bdt, proj, ps, updated_all, hidden_all, pair_grad):
    at = pl.multiple_of(ib * ROWS, ROWS)
    projected(ib, b_l, a_bd, w_bd, proj)
    sides = []
    for first in range(0, ROWS, CHUNK):
        sides += pair_rows(
            at + first, first, pair, cot, proj, bias, gain, shift, wi, wit, wot, updated_all, hidden_all, pair_grad)
    pulled = dot(jnp.concatenate(sides, axis=0), w_bdt[...]).astype(BF16)
    for q in range(16):
        for k in range(NB):
            ps[q * 64 : q * 64 + 64, pl.ds(at + k * 128, 128)] = pulled[k * 64 : k * 64 + 64, q * 128 : q * 128 + 128]


def arrived(ref, sem):
    pltpu.make_async_copy(ref, ref, sem).wait()


def kernel(
    a, b, pair_h, cot_h, weight_h, bias, gain, shift, in_h, out_h,
    new_h, pair_grad_h, grad_a, gb_sum,
    pair, cot, weight, trans_in, trans_out, new_pair, pair_grad,
    a_parts, b_parts, wide, w_bd, w_bdt, wi, wit, wot, b_l, b_lt, a_bd, proj, ps, updated_all, hidden_all,
    ga_out, ga_in, ga_sum, ga_back, gb_out, gb_in,
    load_sem, store_sem, a_send, a_recv, a_first, b_send, b_recv,
    g1_send, g1_recv, g2_send, g2_recv, gb_send, gb_recv,
):
    r, c = lax.axis_index("row"), lax.axis_index("col")
    diagonal = r == c
    off = jnp.logical_not(diagonal)
    remote = functools.partial(pltpu.make_async_remote_copy, device_id_type=MESH)

    loads = [
        pltpu.make_async_copy(x, y, load_sem.at[k])
        for k, (x, y) in enumerate(
            [(weight_h, weight), (in_h, trans_in), (out_h, trans_out), (pair_h, pair), (cot_h, cot)])
    ]
    for copy in loads:
        copy.start()

    barrier = pltpu.get_barrier_semaphore()

    def greet(where):
        pl.semaphore_signal(barrier, inc=1, device_id=where, device_id_type=MESH)

    for k in range(1, PEERS):
        greet(((r + k) % PEERS, c))
        greet((((c + k) % PEERS), r))
        greet((r, (c + k) % PEERS))

    @pl.when(off)
    def _():
        greet((c, r))

    pl.semaphore_wait(barrier, 3 * (PEERS - 1) + off.astype(jnp.int32))

    def b_copy(k):
        return remote(
            src_ref=b, dst_ref=b_parts.at[r], send_sem=b_send, recv_sem=b_recv, device_id=((r + k) % PEERS, c))

    def a_copy(k, ib):
        sem = a_first.at[ib] if k == 0 else a_send.at[ib]
        return remote(
            src_ref=a.at[:, pl.ds(pl.multiple_of(ib * (NB * 64), NB * 64), NB * 64)], dst_ref=a_parts.at[ib, r],
            send_sem=sem, recv_sem=a_recv.at[ib], device_id=(c, (r + k) % PEERS))

    pltpu.make_async_copy(b, b_parts.at[r], b_recv).start()
    for k in range(1, PEERS):
        b_copy(k).start()

    def give_a(ib, _):
        @pl.when(diagonal)
        def _():
            pltpu.make_async_copy(
                a.at[:, pl.ds(pl.multiple_of(ib * (NB * 64), NB * 64), NB * 64)], a_parts.at[ib, r], a_recv.at[ib]).start()

        @pl.when(off)
        def _():
            a_copy(0, ib).start()

        for k in range(1, PEERS):
            a_copy(k, ib).start()
        return 0

    lax.fori_loop(0, BLOCKS, give_a, 0)

    for copy in loads:
        copy.wait()
    prepare_weights(weight, trans_in, trans_out, wide, w_bd, w_bdt, wi, wit, wot)
    arrived(b_parts, b_recv)
    prepare_b(b_parts, wide, b_l, b_lt)

    def g1_copy(k, ib):
        to = (c + k) % PEERS
        return remote(
            src_ref=ga_out.at[ib, to], dst_ref=ga_in.at[ib, c], send_sem=g1_send.at[ib], recv_sem=g1_recv.at[ib],
            device_id=(r, to))

    def g2_copy(ib):
        return remote(
            src_ref=ga_sum.at[ib], dst_ref=ga_back.at[ib], send_sem=g2_send.at[ib], recv_sem=g2_recv.at[ib], device_id=(c, r))

    def combine(ib):
        arrived(ga_in.at[ib], g1_recv.at[ib])
        for m in range(NB // 4):
            ga_sum[ib, :, m * 128 : m * 128 + 128] = jnp.sum(ga_in[ib, :, :, m * 128 : m * 128 + 128].astype(F32), axis=0)

        @pl.when(diagonal)
        def _():
            pltpu.make_async_copy(ga_sum.at[ib], ga_back.at[ib], g2_recv.at[ib]).start()

        @pl.when(off)
        def _():
            g2_copy(ib).start()

    def store(x, y, ib, k):
        part = pl.ds(pl.multiple_of(ib * (NB * 128), NB * 128), NB * 128)
        return pltpu.make_async_copy(x.at[part], y.at[part], store_sem.at[k, ib])

    def step(ib, _):
        arrived(a_parts.at[ib], a_recv.at[ib])
        at = pl.multiple_of(ib * (NB * 128), NB * 128)
        for k in range(NB // 2):
            prepare_a(a_parts[ib, :, :, k * 128 : k * 128 + 128], a_bd, at + k * 256)
        pair_block(
            ib, pair, cot, bias, gain, shift, wi, wit, wot, b_l, a_bd, w_bd, w_bdt, proj, ps, updated_all, hidden_all, pair_grad)
        store(pair_grad, pair_grad_h, ib, 1).start()
        for k in range(2):
            pieces = fold(dot(b_lt[...], ps[:, pl.ds(at + k * (NB * 64), NB * 64)]), NB // 2)
            for m, piece in enumerate(pieces):
                ga_out[ib, :, k * 8 : k * 8 + 8, m * 128 : m * 128 + 128] = piece.reshape(PEERS, 8, 128).astype(BF16)
        pltpu.make_async_copy(ga_out.at[ib, c], ga_in.at[ib, c], g1_recv.at[ib]).start()
        for k in range(1, PEERS):
            g1_copy(k, ib).start()

        @pl.when(ib >= 2)
        def _():
            combine(ib - 2)

        return 0

    lax.fori_loop(0, BLOCKS, step, 0)

    def gb_copy(k, h):
        to = (r + k) % PEERS
        return remote(
            src_ref=gb_out.at[h, to], dst_ref=gb_in.at[h, r], send_sem=gb_send.at[h], recv_sem=gb_recv.at[h],
            device_id=(to, c))

    for h in range(2):
        g = dot_last(a_bd[...], ps[h * 512 : h * 512 + 512, :])
        two = [g[p * 128 : p * 128 + 128].reshape(PEERS, 8, 512) for p in range(2)]
        gb_out[h] = jnp.concatenate(two, axis=1).astype(BF16)
        pltpu.make_async_copy(gb_out.at[h, r], gb_in.at[h, r], gb_recv.at[h]).start()
        for k in range(1, PEERS):
            gb_copy(k, h).start()
    combine(BLOCKS - 2)

    def finish_new(ib, _):
        here = pl.ds(pl.multiple_of(ib * ROWS, ROWS), ROWS)
        new_pair[here, :] = (updated_all[here, :] + dot(hidden_all[here, :], trans_out[...])).astype(BF16)
        store(new_pair, new_h, ib, 0).start()
        return 0

    lax.fori_loop(0, BLOCKS, finish_new, 0)
    combine(BLOCKS - 1)

    for h in range(2):
        arrived(gb_in.at[h], gb_recv.at[h])
        for t in range(4):
            gb_sum[:, h * 512 + t * 128 : h * 512 + t * 128 + 128] = jnp.sum(
                gb_in[h, :, :, t * 128 : t * 128 + 128].astype(F32), axis=0)

    for ib in range(BLOCKS):
        arrived(ga_back.at[ib], g2_recv.at[ib])
        for k in range(2):
            at = ib * (NB * 64) + k * (NB * 32)
            grad_a[:, at : at + NB * 32] = ga_back[ib, k * 8 : k * 8 + 8, :]

    arrived(b_parts.at[0 : PEERS - 1], b_send)
    for h in range(2):
        arrived(gb_out.at[h, 0 : PEERS - 1], gb_send.at[h])
    for ib in range(BLOCKS):
        arrived(a_parts.at[ib, 0 : PEERS - 1], a_send.at[ib])
        arrived(ga_out.at[ib, 0 : PEERS - 1], g1_send.at[ib])
        store(new_pair, new_h, ib, 0).wait()
        store(pair_grad, pair_grad_h, ib, 1).wait()

        @pl.when(off)
        def _(ib=ib):
            a_copy(0, ib).wait_send()
            g2_copy(ib).wait_send()


def finish_kernel(new_h, pair_grad_h, grad_a_h, gb_sum, new_o, pair_grad_o, grad_a_o, grad_b, new, pair_grad, grad_a, wide, in_sem, out_sem):
    pieces = []
    for k in range(4):
        part = slice(k * 1024, k * 1024 + 1024)
        pieces += [(new_h, new, new_o, part), (pair_grad_h, pair_grad, pair_grad_o, part)]
    pieces.append((grad_a_h, grad_a, grad_a_o, slice(0, 8)))
    ins = [pltpu.make_async_copy(x.at[p], y.at[p], in_sem.at[k]) for k, (x, y, _, p) in enumerate(pieces)]
    outs = [pltpu.make_async_copy(y.at[p], z.at[p], out_sem.at[k]) for k, (_, y, z, p) in enumerate(pieces)]
    for copy in ins:
        copy.start()
    for before, after in zip(ins, outs):
        before.wait()
        after.start()
    for t in range(8):
        across = jnp.concatenate([gb_sum[:, t * 128 : t * 128 + 128], jnp.zeros((112, 128), F32)], axis=0).T
        for k in range(2):
            q = 2 * t + k
            rows = across[k * 64 : k * 64 + 64]
            wide[pl.ds(q, 64, stride=32), :] = rows
            wide[pl.ds(16 + q, 64, stride=32), :] = pltpu.roll(rows, 120, 1)
    for t in range(16):
        grad_b[:, t * 128 : t * 128 + 128] = wide[t * 128 : t * 128 + 128, :].T[0:8]
    for copy in outs:
        copy.wait()


def body(factor_a, factor_b, pair, proj_weight, proj_bias, norm_gain, norm_bias, trans_in, trans_out, cotangent):
    S = jax.ShapeDtypeStruct
    vmem = pl.BlockSpec(memory_space=pltpu.VMEM)
    hbm = pl.BlockSpec(memory_space=pl.ANY)
    V = pltpu.VMEM
    D = pltpu.SemaphoreType.DMA
    new_pair, pair_grad, grad_a, gb_sum = pl.pallas_call(
        kernel,
        out_shape=(S((4096, 128), BF16), S((4096, 128), BF16), S((8, 2048), F32), S((16, 1024), F32)),
        in_specs=[vmem, vmem, hbm, hbm, hbm, vmem, vmem, vmem, hbm, hbm],
        out_specs=(hbm, hbm, vmem, vmem),
        scratch_shapes=[
            V((4096, 128), BF16), V((4096, 128), BF16), V((1024, 128), BF16), V((128, 1024), BF16), V((512, 128), BF16),
            V((4096, 128), BF16), V((4096, 128), BF16),
            V((BLOCKS, PEERS, 8, NB * 64), BF16), V((PEERS, 8, 2048), BF16),
            V((2048, 128), F32), V((2048, 256), BF16), V((256, 2048), BF16),
            V((128, 1024), BF16), V((1024, 128), BF16), V((128, 512), BF16),
            V((1024, 256), BF16), V((256, 1024), BF16), V((256, 4096), BF16),
            V((NB * 64, 256), F32), V((1024, 4096), BF16), V((4096, 128), F32), V((4096, 512), BF16),
            V((BLOCKS, PEERS, 16, NB * 32), BF16), V((BLOCKS, PEERS, 16, NB * 32), BF16),
            V((BLOCKS, 16, NB * 32), F32), V((BLOCKS, 16, NB * 32), F32),
            V((2, PEERS, 16, 512), BF16), V((2, PEERS, 16, 512), BF16),
            D((5,)), D((2, BLOCKS)), D((BLOCKS,)), D((BLOCKS,)), D((BLOCKS,)), D, D,
            D((BLOCKS,)), D((BLOCKS,)), D((BLOCKS,)), D((BLOCKS,)), D((2,)), D((2,)),
        ],
        compiler_params=pltpu.CompilerParams(collective_id=0, has_side_effects=True, vmem_limit_bytes=58 << 20),
        name="whole",
    )(
        factor_a, factor_b, pair.reshape(4096, 128), cotangent.reshape(4096, 128), proj_weight,
        proj_bias.reshape(1, 128), norm_gain.reshape(1, 128), norm_bias.reshape(1, 128), trans_in, trans_out)
    new_pair, pair_grad, grad_a, grad_b = pl.pallas_call(
        finish_kernel,
        out_shape=(S((4096, 128), BF16), S((4096, 128), BF16), S((8, 2048), F32), S((8, 2048), F32)),
        in_specs=[hbm, hbm, hbm, vmem],
        out_specs=(hbm, hbm, hbm, vmem),
        scratch_shapes=[V((4096, 128), BF16), V((4096, 128), BF16), V((8, 2048), F32), V((2048, 128), F32), D((9,)), D((9,))],
        name="finish",
    )(new_pair, pair_grad, grad_a, gb_sum)
    return new_pair.reshape(pair.shape), pair_grad.reshape(pair.shape), grad_a, grad_b


def solution(mesh):
    tiles = P("row", "col", None)
    return jax.shard_map(
        body,
        mesh=mesh,
        in_specs=(P("row", "col"), P("row", "col"), tiles, P(), P(), P(), P(), P(), P(), tiles),
        out_specs=(tiles, tiles, P("row", "col"), P("row", "col")),
        check_vma=False,
    )
```

```python
import functools
import jax
import jax.numpy as jnp
from jax import lax
from jax.experimental import pallas as pl
from jax.experimental.pallas import tpu as pltpu
from jax.sharding import PartitionSpec as P

F32, BF16 = jnp.float32, jnp.bfloat16


def dot(x, y):
    return jnp.dot(x, y, preferred_element_type=F32)


def turned(x):
    return x.astype(F32).T.astype(BF16)


def prepare_weights(proj_weight, trans_in, trans_out, wide, w_bd, w_bdt, wi, wit, wot):
    wide[0:1024, :] = proj_weight[...].astype(F32) * (1.0 / 128)
    w_bd[...] = jnp.zeros(w_bd.shape, BF16)
    for q in range(16):
        for p in range(2):
            piece = wide[pl.ds(p * 16 + q, 32, stride=32), :].astype(BF16)
            for k in range(2):
                w_bd[q * 128 + p * 64 + k * 32 : q * 128 + p * 64 + k * 32 + 32, k * 128 : k * 128 + 128] = piece
    for q in range(16):
        w_bdt[:, q * 128 : q * 128 + 128] = turned(w_bd[q * 128 : q * 128 + 128, :])
    wi[:, 0:512] = (trans_in[:, 0:512].astype(F32) * 0.5).astype(BF16)
    wi[:, 512:1024] = trans_in[:, 512:1024]
    for q in range(8):
        wit[q * 128 : q * 128 + 128, :] = turned(wi[:, q * 128 : q * 128 + 128])
    for q in range(4):
        wot[:, q * 128 : q * 128 + 128] = turned(trans_out[q * 128 : q * 128 + 128, :])


def prepare_b(b_parts, wide, b_l, b_lt):
    for q in range(16):
        chunk = b_parts[:, :, q * 128 : q * 128 + 128].astype(F32).reshape(128, 128)
        wide[q * 128 : q * 128 + 128, :] = chunk.T
    for q in range(16):
        for p in range(2):
            piece = wide[pl.ds(p * 16 + q, 64, stride=32), :]
            b_l[q * 64 : q * 64 + 64, p * 128 : p * 128 + 128] = piece.astype(BF16)
    for q in range(8):
        b_lt[:, q * 128 : q * 128 + 128] = turned(b_l[q * 128 : q * 128 + 128, :])


def prepare_a(a_parts, a_bd, at):
    chunk = a_parts.astype(F32).reshape(128, 128)
    other = pltpu.roll(chunk, 64, 1)
    low = lax.broadcasted_iota(jnp.int32, (128, 128), 1) < 64
    zero = jnp.zeros((128, 128), F32)
    a_bd[0:128, pl.ds(at, 128)] = jnp.where(low, chunk, zero).astype(BF16)
    a_bd[128:256, pl.ds(at, 128)] = jnp.where(low, zero, other).astype(BF16)
    a_bd[0:128, pl.ds(at + 128, 128)] = jnp.where(low, other, zero).astype(BF16)
    a_bd[128:256, pl.ds(at + 128, 128)] = jnp.where(low, zero, chunk).astype(BF16)


def fold(y, n):
    out = []
    low = lax.broadcasted_iota(jnp.int32, (128, 128), 1) < 64
    for m in range(0, n, 2):
        e0 = y[0:128, m * 128 : m * 128 + 128]
        e1 = y[128:256, m * 128 : m * 128 + 128]
        o0 = y[0:128, m * 128 + 128 : m * 128 + 256]
        o1 = y[128:256, m * 128 + 128 : m * 128 + 256]
        out.append(jnp.where(low, e0, o1) + pltpu.roll(jnp.where(low, o0, e1), 64, 1))
    return out


MESH = pl.DeviceIdType.MESH
NB = 8
BLOCKS = 32 // NB
ROWS = NB * 128
CHUNK = 256
PEERS = 16


def dot_last(x, y):
    return lax.dot_general(x, y, (((1,), (1,)), ((), ())), preferred_element_type=F32)


def projected(ib, b_l, a_bd, w_bd, proj):
    at = pl.multiple_of(ib * ROWS, ROWS)
    for c in range(4):
        x = dot(b_l[c * 256 : c * 256 + 256, :], a_bd[:, pl.ds(at, ROWS)]).astype(BF16)
        x = jnp.concatenate(
            [
                jnp.concatenate([x[q * 64 : q * 64 + 64, k * 128 : k * 128 + 128] for q in range(4)], axis=1)
                for k in range(NB)
            ],
            axis=0)
        part = dot(x, w_bd[c * 512 : c * 512 + 512, :])
        if c == 0:
            proj[...] = part
        else:
            proj[...] += part


def pair_rows(at, first, pair, cot, proj, bias, gain, shift, wi, wit, wot, updated_all, hidden_all, pair_grad):
    here = pl.ds(at, CHUNK)
    parts = [
        proj[(k // 2) * 64 : (k // 2) * 64 + 64, (k % 2) * 128 : (k % 2) * 128 + 128]
        for k in range(first // 64, (first + CHUNK) // 64)
    ]
    updated = pair[here, :].astype(F32) + (jnp.concatenate(parts, axis=0) + bias[...])
    updated_all[here, :] = updated
    mu = jnp.mean(updated, axis=-1, keepdims=True)
    centered = updated - mu
    var = jnp.mean(centered * centered, axis=-1, keepdims=True)
    inv = lax.rsqrt(var + 1e-05)
    normed = centered * inv
    ln = (normed * gain[...] + shift[...]).astype(BF16)
    cot_here = cot[here, :]
    half = dot(ln, wi[:, 0:512])
    up = dot(ln, wi[:, 512:1024])
    dh = dot(cot_here, wot[...])
    q = 1.0 + jnp.tanh(half)
    act = half * q
    hidden_all[here, :] = (act * up).astype(BF16)
    d_up = (dh * act).astype(BF16)
    d_gate = (dh * up * (q + act * (2.0 - q))).astype(BF16)
    dn = dot(jnp.concatenate([d_gate, d_up], axis=1), wit[...]) * gain[...]
    m1 = jnp.mean(dn, axis=-1, keepdims=True)
    m2 = jnp.mean(dn * normed, axis=-1, keepdims=True)
    g = (cot_here.astype(F32) + inv * (dn - m1 - normed * m2)).astype(BF16)
    pair_grad[here, :] = g
    return [
        jnp.concatenate([g[k * 128 : k * 128 + 64], g[k * 128 + 64 : k * 128 + 128]], axis=1) for k in range(CHUNK // 128)
    ]


def pair_block(ib, pair, cot, bias, gain, shift, wi, wit, wot, b_l, a_bd, w_bd, w_bdt, proj, ps, updated_all, hidden_all, pair_grad):
    at = pl.multiple_of(ib * ROWS, ROWS)
    projected(ib, b_l, a_bd, w_bd, proj)
    sides = []
    for first in range(0, ROWS, CHUNK):
        sides += pair_rows(
            at + first, first, pair, cot, proj, bias, gain, shift, wi, wit, wot, updated_all, hidden_all, pair_grad)
    pulled = dot(jnp.concatenate(sides, axis=0), w_bdt[...]).astype(BF16)
    for q in range(16):
        for k in range(NB):
            ps[q * 64 : q * 64 + 64, pl.ds(at + k * 128, 128)] = pulled[k * 64 : k * 64 + 64, q * 128 : q * 128 + 128]


def arrived(ref, sem):
    pltpu.make_async_copy(ref, ref, sem).wait()


def kernel(
    a, b, pair_h, cot_h, weight_h, bias, gain, shift, in_h, out_h,
    new_h, pair_grad_h, grad_a, gb_sum,
    pair, cot, weight, trans_in, trans_out, new_pair, pair_grad,
    a_parts, b_parts, wide, w_bd, w_bdt, wi, wit, wot, b_l, b_lt, a_bd, proj, ps, updated_all, hidden_all,
    ga_out, ga_in, ga_sum, ga_back, gb_out, gb_in,
    load_sem, store_sem, a_send, a_recv, a_first, b_send, b_recv,
    g1_send, g1_recv, g2_send, g2_recv, gb_send, gb_recv,
):
    r, c = lax.axis_index("row"), lax.axis_index("col")
    diagonal = r == c
    off = jnp.logical_not(diagonal)
    remote = functools.partial(pltpu.make_async_remote_copy, device_id_type=MESH)

    loads = [
        pltpu.make_async_copy(x, y, load_sem.at[k])
        for k, (x, y) in enumerate(
            [(weight_h, weight), (in_h, trans_in), (out_h, trans_out), (pair_h, pair), (cot_h, cot)])
    ]
    for copy in loads:
        copy.start()

    barrier = pltpu.get_barrier_semaphore()

    def greet(where):
        pl.semaphore_signal(barrier, inc=1, device_id=where, device_id_type=MESH)

    for k in range(1, PEERS):
        greet(((r + k) % PEERS, c))
        greet((((c + k) % PEERS), r))
        greet((r, (c + k) % PEERS))

    @pl.when(off)
    def _():
        greet((c, r))

    pl.semaphore_wait(barrier, 3 * (PEERS - 1) + off.astype(jnp.int32))

    def b_copy(k):
        return remote(
            src_ref=b, dst_ref=b_parts.at[r], send_sem=b_send, recv_sem=b_recv, device_id=((r + k) % PEERS, c))

    def a_copy(k, ib):
        sem = a_first.at[ib] if k == 0 else a_send.at[ib]
        return remote(
            src_ref=a.at[:, pl.ds(pl.multiple_of(ib * (NB * 64), NB * 64), NB * 64)], dst_ref=a_parts.at[ib, r],
            send_sem=sem, recv_sem=a_recv.at[ib], device_id=(c, (r + k) % PEERS))

    def give_a(ib, _):
        @pl.when(diagonal)
        def _():
            pltpu.make_async_copy(
                a.at[:, pl.ds(pl.multiple_of(ib * (NB * 64), NB * 64), NB * 64)], a_parts.at[ib, r], a_recv.at[ib]).start()

        @pl.when(off)
        def _():
            a_copy(0, ib).start()

        for k in range(1, PEERS):
            a_copy(k, ib).start()
        return 0

    give_a(0, 0)
    pltpu.make_async_copy(b, b_parts.at[r], b_recv).start()
    for k in range(1, PEERS):
        b_copy(k).start()
    lax.fori_loop(1, BLOCKS, give_a, 0)

    for copy in loads:
        copy.wait()
    prepare_weights(weight, trans_in, trans_out, wide, w_bd, w_bdt, wi, wit, wot)
    arrived(b_parts, b_recv)
    prepare_b(b_parts, wide, b_l, b_lt)

    def g1_copy(k, ib):
        to = (c + k) % PEERS
        return remote(
            src_ref=ga_out.at[ib, to], dst_ref=ga_in.at[ib, c], send_sem=g1_send.at[ib], recv_sem=g1_recv.at[ib],
            device_id=(r, to))

    def g2_copy(ib):
        return remote(
            src_ref=ga_sum.at[ib], dst_ref=ga_back.at[ib], send_sem=g2_send.at[ib], recv_sem=g2_recv.at[ib], device_id=(c, r))

    def combine(ib):
        arrived(ga_in.at[ib], g1_recv.at[ib])
        for m in range(NB // 4):
            ga_sum[ib, :, m * 128 : m * 128 + 128] = jnp.sum(ga_in[ib, :, :, m * 128 : m * 128 + 128].astype(F32), axis=0)

        @pl.when(diagonal)
        def _():
            pltpu.make_async_copy(ga_sum.at[ib], ga_back.at[ib], g2_recv.at[ib]).start()

        @pl.when(off)
        def _():
            g2_copy(ib).start()

    def store(x, y, ib, k):
        part = pl.ds(pl.multiple_of(ib * (NB * 128), NB * 128), NB * 128)
        return pltpu.make_async_copy(x.at[part], y.at[part], store_sem.at[k, ib])

    def step(ib, _):
        arrived(a_parts.at[ib], a_recv.at[ib])
        at = pl.multiple_of(ib * (NB * 128), NB * 128)
        for k in range(NB // 2):
            prepare_a(a_parts[ib, :, :, k * 128 : k * 128 + 128], a_bd, at + k * 256)
        pair_block(
            ib, pair, cot, bias, gain, shift, wi, wit, wot, b_l, a_bd, w_bd, w_bdt, proj, ps, updated_all, hidden_all, pair_grad)
        store(pair_grad, pair_grad_h, ib, 1).start()
        for k in range(2):
            pieces = fold(dot(b_lt[...], ps[:, pl.ds(at + k * (NB * 64), NB * 64)]), NB // 2)
            for m, piece in enumerate(pieces):
                ga_out[ib, :, k * 8 : k * 8 + 8, m * 128 : m * 128 + 128] = piece.reshape(PEERS, 8, 128).astype(BF16)
        pltpu.make_async_copy(ga_out.at[ib, c], ga_in.at[ib, c], g1_recv.at[ib]).start()
        for k in range(1, PEERS):
            g1_copy(k, ib).start()

        @pl.when(ib >= 2)
        def _():
            combine(ib - 2)

        return 0

    lax.fori_loop(0, BLOCKS, step, 0)

    def gb_copy(k, h):
        to = (r + k) % PEERS
        return remote(
            src_ref=gb_out.at[h, to], dst_ref=gb_in.at[h, r], send_sem=gb_send.at[h], recv_sem=gb_recv.at[h],
            device_id=(to, c))

    for h in range(2):
        g = dot_last(a_bd[...], ps[h * 512 : h * 512 + 512, :])
        two = [g[p * 128 : p * 128 + 128].reshape(PEERS, 8, 512) for p in range(2)]
        gb_out[h] = jnp.concatenate(two, axis=1).astype(BF16)
        pltpu.make_async_copy(gb_out.at[h, r], gb_in.at[h, r], gb_recv.at[h]).start()
        for k in range(1, PEERS):
            gb_copy(k, h).start()
    combine(BLOCKS - 2)

    def finish_new(ib, _):
        here = pl.ds(pl.multiple_of(ib * ROWS, ROWS), ROWS)
        new_pair[here, :] = (updated_all[here, :] + dot(hidden_all[here, :], trans_out[...])).astype(BF16)
        store(new_pair, new_h, ib, 0).start()
        return 0

    lax.fori_loop(0, BLOCKS, finish_new, 0)
    combine(BLOCKS - 1)

    for h in range(2):
        arrived(gb_in.at[h], gb_recv.at[h])
        for t in range(4):
            gb_sum[:, h * 512 + t * 128 : h * 512 + t * 128 + 128] = jnp.sum(
                gb_in[h, :, :, t * 128 : t * 128 + 128].astype(F32), axis=0)

    for ib in range(BLOCKS):
        arrived(ga_back.at[ib], g2_recv.at[ib])
        for k in range(2):
            at = ib * (NB * 64) + k * (NB * 32)
            grad_a[:, at : at + NB * 32] = ga_back[ib, k * 8 : k * 8 + 8, :]

    arrived(b_parts.at[0 : PEERS - 1], b_send)
    for h in range(2):
        arrived(gb_out.at[h, 0 : PEERS - 1], gb_send.at[h])
    for ib in range(BLOCKS):
        arrived(a_parts.at[ib, 0 : PEERS - 1], a_send.at[ib])
        arrived(ga_out.at[ib, 0 : PEERS - 1], g1_send.at[ib])
        store(new_pair, new_h, ib, 0).wait()
        store(pair_grad, pair_grad_h, ib, 1).wait()

        @pl.when(off)
        def _(ib=ib):
            a_copy(0, ib).wait_send()
            g2_copy(ib).wait_send()


def finish_kernel(new_h, pair_grad_h, grad_a_h, gb_sum, new_o, pair_grad_o, grad_a_o, grad_b, new, pair_grad, grad_a, wide, in_sem, out_sem):
    pieces = []
    for k in range(4):
        part = slice(k * 1024, k * 1024 + 1024)
        pieces += [(new_h, new, new_o, part), (pair_grad_h, pair_grad, pair_grad_o, part)]
    pieces.append((grad_a_h, grad_a, grad_a_o, slice(0, 8)))
    ins = [pltpu.make_async_copy(x.at[p], y.at[p], in_sem.at[k]) for k, (x, y, _, p) in enumerate(pieces)]
    outs = [pltpu.make_async_copy(y.at[p], z.at[p], out_sem.at[k]) for k, (_, y, z, p) in enumerate(pieces)]
    for copy in ins:
        copy.start()
    for t in range(8):
        across = jnp.concatenate([gb_sum[:, t * 128 : t * 128 + 128], jnp.zeros((112, 128), F32)], axis=0).T
        for k in range(2):
            q = 2 * t + k
            rows = across[k * 64 : k * 64 + 64]
            wide[pl.ds(q, 64, stride=32), :] = rows
            wide[pl.ds(16 + q, 64, stride=32), :] = pltpu.roll(rows, 120, 1)
    for before, after in zip(ins, outs):
        before.wait()
        after.start()
    for t in range(16):
        grad_b[:, t * 128 : t * 128 + 128] = wide[t * 128 : t * 128 + 128, :].T[0:8]
    for copy in outs:
        copy.wait()


def body(factor_a, factor_b, pair, proj_weight, proj_bias, norm_gain, norm_bias, trans_in, trans_out, cotangent):
    S = jax.ShapeDtypeStruct
    vmem = pl.BlockSpec(memory_space=pltpu.VMEM)
    hbm = pl.BlockSpec(memory_space=pl.ANY)
    V = pltpu.VMEM
    D = pltpu.SemaphoreType.DMA
    new_pair, pair_grad, grad_a, gb_sum = pl.pallas_call(
        kernel,
        out_shape=(S((4096, 128), BF16), S((4096, 128), BF16), S((8, 2048), F32), S((16, 1024), F32)),
        in_specs=[vmem, vmem, hbm, hbm, hbm, vmem, vmem, vmem, hbm, hbm],
        out_specs=(hbm, hbm, vmem, vmem),
        scratch_shapes=[
            V((4096, 128), BF16), V((4096, 128), BF16), V((1024, 128), BF16), V((128, 1024), BF16), V((512, 128), BF16),
            V((4096, 128), BF16), V((4096, 128), BF16),
            V((BLOCKS, PEERS, 8, NB * 64), BF16), V((PEERS, 8, 2048), BF16),
            V((2048, 128), F32), V((2048, 256), BF16), V((256, 2048), BF16),
            V((128, 1024), BF16), V((1024, 128), BF16), V((128, 512), BF16),
            V((1024, 256), BF16), V((256, 1024), BF16), V((256, 4096), BF16),
            V((NB * 64, 256), F32), V((1024, 4096), BF16), V((4096, 128), F32), V((4096, 512), BF16),
            V((BLOCKS, PEERS, 16, NB * 32), BF16), V((BLOCKS, PEERS, 16, NB * 32), BF16),
            V((BLOCKS, 16, NB * 32), F32), V((BLOCKS, 16, NB * 32), F32),
            V((2, PEERS, 16, 512), BF16), V((2, PEERS, 16, 512), BF16),
            D((5,)), D((2, BLOCKS)), D((BLOCKS,)), D((BLOCKS,)), D((BLOCKS,)), D, D,
            D((BLOCKS,)), D((BLOCKS,)), D((BLOCKS,)), D((BLOCKS,)), D((2,)), D((2,)),
        ],
        compiler_params=pltpu.CompilerParams(collective_id=0, has_side_effects=True, vmem_limit_bytes=58 << 20),
        name="whole",
    )(
        factor_a, factor_b, pair.reshape(4096, 128), cotangent.reshape(4096, 128), proj_weight,
        proj_bias.reshape(1, 128), norm_gain.reshape(1, 128), norm_bias.reshape(1, 128), trans_in, trans_out)
    new_pair, pair_grad, grad_a, grad_b = pl.pallas_call(
        finish_kernel,
        out_shape=(S((4096, 128), BF16), S((4096, 128), BF16), S((8, 2048), F32), S((8, 2048), F32)),
        in_specs=[hbm, hbm, hbm, vmem],
        out_specs=(hbm, hbm, hbm, vmem),
        scratch_shapes=[V((4096, 128), BF16), V((4096, 128), BF16), V((8, 2048), F32), V((2048, 128), F32), D((9,)), D((9,))],
        name="finish",
    )(new_pair, pair_grad, grad_a, gb_sum)
    return new_pair.reshape(pair.shape), pair_grad.reshape(pair.shape), grad_a, grad_b


def solution(mesh):
    tiles = P("row", "col", None)
    return jax.shard_map(
        body,
        mesh=mesh,
        in_specs=(P("row", "col"), P("row", "col"), tiles, P(), P(), P(), P(), P(), P(), tiles),
        out_specs=(tiles, tiles, P("row", "col"), P("row", "col")),
        check_vma=False,
    )
```

```python
import functools
import jax
import jax.numpy as jnp
from jax import lax
from jax.experimental import pallas as pl
from jax.experimental.pallas import tpu as pltpu
from jax.sharding import PartitionSpec as P

F32, BF16 = jnp.float32, jnp.bfloat16


def dot(x, y):
    return jnp.dot(x, y, preferred_element_type=F32)


def turned(x):
    return x.astype(F32).T.astype(BF16)


def prepare_weights(proj_weight, trans_in, trans_out, wide, w_bd, w_bdt, wi, wit, wot):
    wide[0:1024, :] = proj_weight[...].astype(F32) * (1.0 / 128)
    w_bd[...] = jnp.zeros(w_bd.shape, BF16)
    for q in range(16):
        for p in range(2):
            piece = wide[pl.ds(p * 16 + q, 32, stride=32), :].astype(BF16)
            for k in range(2):
                w_bd[q * 128 + p * 64 + k * 32 : q * 128 + p * 64 + k * 32 + 32, k * 128 : k * 128 + 128] = piece
    for q in range(16):
        w_bdt[:, q * 128 : q * 128 + 128] = turned(w_bd[q * 128 : q * 128 + 128, :])
    wi[:, 0:512] = (trans_in[:, 0:512].astype(F32) * 0.5).astype(BF16)
    wi[:, 512:1024] = trans_in[:, 512:1024]
    for q in range(8):
        wit[q * 128 : q * 128 + 128, :] = turned(wi[:, q * 128 : q * 128 + 128])
    for q in range(4):
        wot[:, q * 128 : q * 128 + 128] = turned(trans_out[q * 128 : q * 128 + 128, :])


def prepare_b(b_parts, wide, b_l, b_lt):
    for q in range(16):
        chunk = b_parts[:, :, q * 128 : q * 128 + 128].astype(F32).reshape(128, 128)
        wide[q * 128 : q * 128 + 128, :] = chunk.T
    for q in range(16):
        for p in range(2):
            piece = wide[pl.ds(p * 16 + q, 64, stride=32), :]
            b_l[q * 64 : q * 64 + 64, p * 128 : p * 128 + 128] = piece.astype(BF16)
    for q in range(8):
        b_lt[:, q * 128 : q * 128 + 128] = turned(b_l[q * 128 : q * 128 + 128, :])


def prepare_a(a_parts, a_bd, at):
    chunk = a_parts.astype(F32).reshape(128, 128)
    other = pltpu.roll(chunk, 64, 1)
    low = lax.broadcasted_iota(jnp.int32, (128, 128), 1) < 64
    zero = jnp.zeros((128, 128), F32)
    a_bd[0:128, pl.ds(at, 128)] = jnp.where(low, chunk, zero).astype(BF16)
    a_bd[128:256, pl.ds(at, 128)] = jnp.where(low, zero, other).astype(BF16)
    a_bd[0:128, pl.ds(at + 128, 128)] = jnp.where(low, other, zero).astype(BF16)
    a_bd[128:256, pl.ds(at + 128, 128)] = jnp.where(low, zero, chunk).astype(BF16)


def fold(y, n):
    out = []
    low = lax.broadcasted_iota(jnp.int32, (128, 128), 1) < 64
    for m in range(0, n, 2):
        e0 = y[0:128, m * 128 : m * 128 + 128]
        e1 = y[128:256, m * 128 : m * 128 + 128]
        o0 = y[0:128, m * 128 + 128 : m * 128 + 256]
        o1 = y[128:256, m * 128 + 128 : m * 128 + 256]
        out.append(jnp.where(low, e0, o1) + pltpu.roll(jnp.where(low, o0, e1), 64, 1))
    return out


MESH = pl.DeviceIdType.MESH
NB = 16
BLOCKS = 32 // NB
ROWS = NB * 128
CHUNK = 256
PEERS = 16


def dot_last(x, y):
    return lax.dot_general(x, y, (((1,), (1,)), ((), ())), preferred_element_type=F32)


def projected(ib, b_l, a_bd, w_bd, proj):
    at = pl.multiple_of(ib * ROWS, ROWS)
    for c in range(4):
        x = dot(b_l[c * 256 : c * 256 + 256, :], a_bd[:, pl.ds(at, ROWS)]).astype(BF16)
        x = jnp.concatenate(
            [
                jnp.concatenate([x[q * 64 : q * 64 + 64, k * 128 : k * 128 + 128] for q in range(4)], axis=1)
                for k in range(NB)
            ],
            axis=0)
        part = dot(x, w_bd[c * 512 : c * 512 + 512, :])
        if c == 0:
            proj[...] = part
        else:
            proj[...] += part


def pair_rows(at, first, pair, cot, proj, bias, gain, shift, wi, wit, wot, updated_all, hidden_all, pair_grad):
    here = pl.ds(at, CHUNK)
    parts = [
        proj[(k // 2) * 64 : (k // 2) * 64 + 64, (k % 2) * 128 : (k % 2) * 128 + 128]
        for k in range(first // 64, (first + CHUNK) // 64)
    ]
    updated = pair[here, :].astype(F32) + (jnp.concatenate(parts, axis=0) + bias[...])
    updated_all[here, :] = updated
    mu = jnp.mean(updated, axis=-1, keepdims=True)
    centered = updated - mu
    var = jnp.mean(centered * centered, axis=-1, keepdims=True)
    inv = lax.rsqrt(var + 1e-05)
    normed = centered * inv
    ln = (normed * gain[...] + shift[...]).astype(BF16)
    cot_here = cot[here, :]
    half = dot(ln, wi[:, 0:512])
    up = dot(ln, wi[:, 512:1024])
    dh = dot(cot_here, wot[...])
    q = 1.0 + jnp.tanh(half)
    act = half * q
    hidden_all[here, :] = (act * up).astype(BF16)
    d_up = (dh * act).astype(BF16)
    d_gate = (dh * up * (q + act * (2.0 - q))).astype(BF16)
    dn = dot(jnp.concatenate([d_gate, d_up], axis=1), wit[...]) * gain[...]
    m1 = jnp.mean(dn, axis=-1, keepdims=True)
    m2 = jnp.mean(dn * normed, axis=-1, keepdims=True)
    g = (cot_here.astype(F32) + inv * (dn - m1 - normed * m2)).astype(BF16)
    pair_grad[here, :] = g
    return [
        jnp.concatenate([g[k * 128 : k * 128 + 64], g[k * 128 + 64 : k * 128 + 128]], axis=1) for k in range(CHUNK // 128)
    ]


def pair_block(ib, pair, cot, bias, gain, shift, wi, wit, wot, b_l, a_bd, w_bd, w_bdt, proj, ps, updated_all, hidden_all, pair_grad):
    at = pl.multiple_of(ib * ROWS, ROWS)
    projected(ib, b_l, a_bd, w_bd, proj)
    sides = []
    for first in range(0, ROWS, CHUNK):
        sides += pair_rows(
            at + first, first, pair, cot, proj, bias, gain, shift, wi, wit, wot, updated_all, hidden_all, pair_grad)
    pulled = dot(jnp.concatenate(sides, axis=0), w_bdt[...]).astype(BF16)
    for q in range(16):
        for k in range(NB):
            ps[q * 64 : q * 64 + 64, pl.ds(at + k * 128, 128)] = pulled[k * 64 : k * 64 + 64, q * 128 : q * 128 + 128]


def arrived(ref, sem):
    pltpu.make_async_copy(ref, ref, sem).wait()


def kernel(
    a, b, pair_h, cot_h, weight_h, bias, gain, shift, in_h, out_h,
    new_h, pair_grad_h, grad_a, gb_sum,
    pair, cot, weight, trans_in, trans_out, new_pair, pair_grad,
    a_parts, b_parts, wide, w_bd, w_bdt, wi, wit, wot, b_l, b_lt, a_bd, proj, ps, updated_all, hidden_all,
    ga_out, ga_in, ga_sum, ga_back, gb_out, gb_in,
    load_sem, store_sem, a_send, a_recv, a_first, b_send, b_recv,
    g1_send, g1_recv, g2_send, g2_recv, gb_send, gb_recv,
):
    r, c = lax.axis_index("row"), lax.axis_index("col")
    diagonal = r == c
    off = jnp.logical_not(diagonal)
    remote = functools.partial(pltpu.make_async_remote_copy, device_id_type=MESH)

    loads = [
        pltpu.make_async_copy(x, y, load_sem.at[k])
        for k, (x, y) in enumerate(
            [(weight_h, weight), (in_h, trans_in), (out_h, trans_out), (pair_h, pair), (cot_h, cot)])
    ]
    for copy in loads:
        copy.start()

    barrier = pltpu.get_barrier_semaphore()

    def greet(where):
        pl.semaphore_signal(barrier, inc=1, device_id=where, device_id_type=MESH)

    for k in range(1, PEERS):
        greet(((r + k) % PEERS, c))
        greet((((c + k) % PEERS), r))
        greet((r, (c + k) % PEERS))

    @pl.when(off)
    def _():
        greet((c, r))

    pl.semaphore_wait(barrier, 3 * (PEERS - 1) + off.astype(jnp.int32))

    def b_copy(k):
        return remote(
            src_ref=b, dst_ref=b_parts.at[r], send_sem=b_send, recv_sem=b_recv, device_id=((r + k) % PEERS, c))

    def a_copy(k, ib):
        sem = a_first.at[ib] if k == 0 else a_send.at[ib]
        return remote(
            src_ref=a.at[:, pl.ds(pl.multiple_of(ib * (NB * 64), NB * 64), NB * 64)], dst_ref=a_parts.at[ib, r],
            send_sem=sem, recv_sem=a_recv.at[ib], device_id=(c, (r + k) % PEERS))

    pltpu.make_async_copy(b, b_parts.at[r], b_recv).start()
    for k in range(1, PEERS):
        b_copy(k).start()

    def give_a(ib, _):
        @pl.when(diagonal)
        def _():
            pltpu.make_async_copy(
                a.at[:, pl.ds(pl.multiple_of(ib * (NB * 64), NB * 64), NB * 64)], a_parts.at[ib, r], a_recv.at[ib]).start()

        @pl.when(off)
        def _():
            a_copy(0, ib).start()

        for k in range(1, PEERS):
            a_copy(k, ib).start()
        return 0

    lax.fori_loop(0, BLOCKS, give_a, 0)

    for copy in loads:
        copy.wait()
    prepare_weights(weight, trans_in, trans_out, wide, w_bd, w_bdt, wi, wit, wot)
    arrived(b_parts, b_recv)
    prepare_b(b_parts, wide, b_l, b_lt)

    def g1_copy(k, ib):
        to = (c + k) % PEERS
        return remote(
            src_ref=ga_out.at[ib, to], dst_ref=ga_in.at[ib, c], send_sem=g1_send.at[ib], recv_sem=g1_recv.at[ib],
            device_id=(r, to))

    def g2_copy(ib):
        return remote(
            src_ref=ga_sum.at[ib], dst_ref=ga_back.at[ib], send_sem=g2_send.at[ib], recv_sem=g2_recv.at[ib], device_id=(c, r))

    def combine(ib):
        arrived(ga_in.at[ib], g1_recv.at[ib])
        for m in range(NB // 4):
            ga_sum[ib, :, m * 128 : m * 128 + 128] = jnp.sum(ga_in[ib, :, :, m * 128 : m * 128 + 128].astype(F32), axis=0)

        @pl.when(diagonal)
        def _():
            pltpu.make_async_copy(ga_sum.at[ib], ga_back.at[ib], g2_recv.at[ib]).start()

        @pl.when(off)
        def _():
            g2_copy(ib).start()

    def store(x, y, ib, k):
        part = pl.ds(pl.multiple_of(ib * (NB * 128), NB * 128), NB * 128)
        return pltpu.make_async_copy(x.at[part], y.at[part], store_sem.at[k, ib])

    def step(ib, _):
        arrived(a_parts.at[ib], a_recv.at[ib])
        at = pl.multiple_of(ib * (NB * 128), NB * 128)
        for k in range(NB // 2):
            prepare_a(a_parts[ib, :, :, k * 128 : k * 128 + 128], a_bd, at + k * 256)
        pair_block(
            ib, pair, cot, bias, gain, shift, wi, wit, wot, b_l, a_bd, w_bd, w_bdt, proj, ps, updated_all, hidden_all, pair_grad)
        store(pair_grad, pair_grad_h, ib, 1).start()
        for k in range(2):
            pieces = fold(dot(b_lt[...], ps[:, pl.ds(at + k * (NB * 64), NB * 64)]), NB // 2)
            for m, piece in enumerate(pieces):
                ga_out[ib, :, k * 8 : k * 8 + 8, m * 128 : m * 128 + 128] = piece.reshape(PEERS, 8, 128).astype(BF16)
        pltpu.make_async_copy(ga_out.at[ib, c], ga_in.at[ib, c], g1_recv.at[ib]).start()
        for k in range(1, PEERS):
            g1_copy(k, ib).start()

        @pl.when(ib >= 2)
        def _():
            combine(ib - 2)

        return 0

    lax.fori_loop(0, BLOCKS, step, 0)

    def gb_copy(k, h):
        to = (r + k) % PEERS
        return remote(
            src_ref=gb_out.at[h, to], dst_ref=gb_in.at[h, r], send_sem=gb_send.at[h], recv_sem=gb_recv.at[h],
            device_id=(to, c))

    for h in range(2):
        g = dot_last(a_bd[...], ps[h * 512 : h * 512 + 512, :])
        two = [g[p * 128 : p * 128 + 128].reshape(PEERS, 8, 512) for p in range(2)]
        gb_out[h] = jnp.concatenate(two, axis=1).astype(BF16)
        pltpu.make_async_copy(gb_out.at[h, r], gb_in.at[h, r], gb_recv.at[h]).start()
        for k in range(1, PEERS):
            gb_copy(k, h).start()
    combine(BLOCKS - 2)

    def finish_new(ib, _):
        here = pl.ds(pl.multiple_of(ib * ROWS, ROWS), ROWS)
        new_pair[here, :] = (updated_all[here, :] + dot(hidden_all[here, :], trans_out[...])).astype(BF16)
        store(new_pair, new_h, ib, 0).start()
        return 0

    lax.fori_loop(0, BLOCKS, finish_new, 0)
    combine(BLOCKS - 1)

    for h in range(2):
        arrived(gb_in.at[h], gb_recv.at[h])
        for t in range(4):
            gb_sum[:, h * 512 + t * 128 : h * 512 + t * 128 + 128] = jnp.sum(
                gb_in[h, :, :, t * 128 : t * 128 + 128].astype(F32), axis=0)

    for ib in range(BLOCKS):
        arrived(ga_back.at[ib], g2_recv.at[ib])
        for k in range(2):
            at = ib * (NB * 64) + k * (NB * 32)
            grad_a[:, at : at + NB * 32] = ga_back[ib, k * 8 : k * 8 + 8, :]

    arrived(b_parts.at[0 : PEERS - 1], b_send)
    for h in range(2):
        arrived(gb_out.at[h, 0 : PEERS - 1], gb_send.at[h])
    for ib in range(BLOCKS):
        arrived(a_parts.at[ib, 0 : PEERS - 1], a_send.at[ib])
        arrived(ga_out.at[ib, 0 : PEERS - 1], g1_send.at[ib])
        store(new_pair, new_h, ib, 0).wait()
        store(pair_grad, pair_grad_h, ib, 1).wait()

        @pl.when(off)
        def _(ib=ib):
            a_copy(0, ib).wait_send()
            g2_copy(ib).wait_send()


def finish_kernel(new_h, pair_grad_h, grad_a_h, gb_sum, new_o, pair_grad_o, grad_a_o, grad_b, new, pair_grad, grad_a, wide, in_sem, out_sem):
    pieces = []
    for k in range(4):
        part = slice(k * 1024, k * 1024 + 1024)
        pieces += [(new_h, new, new_o, part), (pair_grad_h, pair_grad, pair_grad_o, part)]
    pieces.append((grad_a_h, grad_a, grad_a_o, slice(0, 8)))
    ins = [pltpu.make_async_copy(x.at[p], y.at[p], in_sem.at[k]) for k, (x, y, _, p) in enumerate(pieces)]
    outs = [pltpu.make_async_copy(y.at[p], z.at[p], out_sem.at[k]) for k, (_, y, z, p) in enumerate(pieces)]
    for copy in ins:
        copy.start()
    for before, after in zip(ins, outs):
        before.wait()
        after.start()
    for t in range(8):
        across = jnp.concatenate([gb_sum[:, t * 128 : t * 128 + 128], jnp.zeros((112, 128), F32)], axis=0).T
        for k in range(2):
            q = 2 * t + k
            rows = across[k * 64 : k * 64 + 64]
            wide[pl.ds(q, 64, stride=32), :] = rows
            wide[pl.ds(16 + q, 64, stride=32), :] = pltpu.roll(rows, 120, 1)
    for t in range(16):
        grad_b[:, t * 128 : t * 128 + 128] = wide[t * 128 : t * 128 + 128, :].T[0:8]
    for copy in outs:
        copy.wait()


def body(factor_a, factor_b, pair, proj_weight, proj_bias, norm_gain, norm_bias, trans_in, trans_out, cotangent):
    S = jax.ShapeDtypeStruct
    vmem = pl.BlockSpec(memory_space=pltpu.VMEM)
    hbm = pl.BlockSpec(memory_space=pl.ANY)
    V = pltpu.VMEM
    D = pltpu.SemaphoreType.DMA
    new_pair, pair_grad, grad_a, gb_sum = pl.pallas_call(
        kernel,
        out_shape=(S((4096, 128), BF16), S((4096, 128), BF16), S((8, 2048), F32), S((16, 1024), F32)),
        in_specs=[vmem, vmem, hbm, hbm, hbm, vmem, vmem, vmem, hbm, hbm],
        out_specs=(hbm, hbm, vmem, vmem),
        scratch_shapes=[
            V((4096, 128), BF16), V((4096, 128), BF16), V((1024, 128), BF16), V((128, 1024), BF16), V((512, 128), BF16),
            V((4096, 128), BF16), V((4096, 128), BF16),
            V((BLOCKS, PEERS, 8, NB * 64), BF16), V((PEERS, 8, 2048), BF16),
            V((2048, 128), F32), V((2048, 256), BF16), V((256, 2048), BF16),
            V((128, 1024), BF16), V((1024, 128), BF16), V((128, 512), BF16),
            V((1024, 256), BF16), V((256, 1024), BF16), V((256, 4096), BF16),
            V((NB * 64, 256), F32), V((1024, 4096), BF16), V((4096, 128), F32), V((4096, 512), BF16),
            V((BLOCKS, PEERS, 16, NB * 32), BF16), V((BLOCKS, PEERS, 16, NB * 32), BF16),
            V((BLOCKS, 16, NB * 32), F32), V((BLOCKS, 16, NB * 32), F32),
            V((2, PEERS, 16, 512), BF16), V((2, PEERS, 16, 512), BF16),
            D((5,)), D((2, BLOCKS)), D((BLOCKS,)), D((BLOCKS,)), D((BLOCKS,)), D, D,
            D((BLOCKS,)), D((BLOCKS,)), D((BLOCKS,)), D((BLOCKS,)), D((2,)), D((2,)),
        ],
        compiler_params=pltpu.CompilerParams(collective_id=0, has_side_effects=True, vmem_limit_bytes=58 << 20),
        name="whole",
    )(
        factor_a, factor_b, pair.reshape(4096, 128), cotangent.reshape(4096, 128), proj_weight,
        proj_bias.reshape(1, 128), norm_gain.reshape(1, 128), norm_bias.reshape(1, 128), trans_in, trans_out)
    new_pair, pair_grad, grad_a, grad_b = pl.pallas_call(
        finish_kernel,
        out_shape=(S((4096, 128), BF16), S((4096, 128), BF16), S((8, 2048), F32), S((8, 2048), F32)),
        in_specs=[hbm, hbm, hbm, vmem],
        out_specs=(hbm, hbm, hbm, vmem),
        scratch_shapes=[V((4096, 128), BF16), V((4096, 128), BF16), V((8, 2048), F32), V((2048, 128), F32), D((9,)), D((9,))],
        name="finish",
    )(new_pair, pair_grad, grad_a, gb_sum)
    return new_pair.reshape(pair.shape), pair_grad.reshape(pair.shape), grad_a, grad_b


def solution(mesh):
    tiles = P("row", "col", None)
    return jax.shard_map(
        body,
        mesh=mesh,
        in_specs=(P("row", "col"), P("row", "col"), tiles, P(), P(), P(), P(), P(), P(), tiles),
        out_specs=(tiles, tiles, P("row", "col"), P("row", "col")),
        check_vma=False,
    )
```
